128 devices in a mesh: row: 8 (over y, core), grid: 16 (over z, x).
Axes of the slice: x: 4, y: 4, z: 4, core: 2. Of those that a mesh axis runs over, the one named last changes fastest.
Arguments:
- h_rows: bfloat16 [16, 2048, 2048], P('grid', 'row'), may hold values from -6 to 6
- x_blocks: bfloat16 [16, 16, 8, 128, 128], P('grid', 'row'), may hold values from -0.1875 to 0.1875
- x_cols: int32 [16, 16, 8], P('grid', 'row'), may hold values from 0 to 15
- sub_blocks: int32 [8, 16, 3, 6], P('row', 'grid'), may hold values from 0 to 15, as said below
- owners: int32 [8, 16, 3], P('row'), may hold values from 0 to 15, as said below
- shift_mu: float32 [1], replicated, may hold values from -4 to 4
- orbitals: bfloat16 [8, 16, 6, 768, 1536], P('row', 'grid'), may hold values from -0.125 to 0.125
Outputs:
- density: float32 [16, 1024], P('grid', 'row')
The draws below stay inside these ranges and needn't reach their ends.
Inputs may be any that keep to these rules, and one draw needn't show every extreme that they name: `x_cols`: entries of a block row may repeat; repeated blocks add. `sub_blocks`: the 6 blocks of a submatrix are distinct; the first is its central block. Within each row index, a device's 3 submatrices go to distinct owners, and every owner receives 1 to 6 submatrices.
All inputs are finite; a program needn't handle non-finite values.
Results may differ from the reference program's by a relative error of at most 0.0003.
Values may be sent and summed in bfloat16 or wider, within the bound.
A program may use at most 128 MiB of HBM per device.

```python
import jax
import jax.numpy as jnp
from jax import lax

BLK = 128
SUB_BLK = 6
NZ = 8
SUB_DEV = 3
OWN_MAX = 6
PLANE = 256
DEPTH = 4
MARG = 1
ORDER = 768
KB = 16
NREG = 2048
CELLS = 1024
EXT = 1536
N_ROW = 8
N_GRID = 16


owner_table = ((0, 1, 2), (0, 1, 2), (0, 1, 2), (0, 1, 3), (0, 1, 3), (0, 1, 3), (4, 5, 6), (4, 5, 7))


def draw_owners(key, part):

    def single(subkey):
        first, second = jax.random.split(subkey)
        perm_source = jax.random.permutation(first, N_GRID)
        perm_owner = jax.random.permutation(second, N_GRID)
        place = jnp.argsort(perm_source)
        table = jnp.array(owner_table, dtype=jnp.int32)
        within = table[place % 8]
        return perm_owner[(place // 8 * 8)[:, None] + within]
    keys = jax.random.split(jax.random.fold_in(key, 11), N_ROW)
    return jax.vmap(single)(keys).astype(jnp.int32)


def draw_sub_blocks(key, part):
    total = N_ROW * N_GRID * SUB_DEV
    keys = jax.random.split(jax.random.fold_in(key, 23), total)
    picks = jax.vmap(lambda k: jax.random.permutation(k, KB)[:SUB_BLK])(keys)
    return picks.reshape(N_ROW, N_GRID, SUB_DEV, SUB_BLK).astype(jnp.int32)


def with_ends(values, own_key, smallest, high):
    longest = values.shape.index(max(values.shape))
    spots = []
    for shift in (0, 1):
        where = [jax.random.randint(jax.random.fold_in(own_key, axis), (), 0, length) for axis, length in enumerate(values.shape)]
        where[longest] = (where[longest] + shift) % values.shape[longest]
        spots.append(tuple(where))
    return values.at[spots[0]].set(smallest).at[spots[1]].set(high)


def level_of(stream_key, shape, shards, smallest, top_value):
    def one(position, parts):
        heights = jax.random.uniform(jax.random.fold_in(jax.random.fold_in(stream_key, 6), position), (parts,), jnp.float32, smallest / len(shards), top_value / len(shards))
        return jnp.repeat(jnp.exp(heights), shape[position] // parts).reshape((-1,) + (1,) * (len(shape) - position - 1))

    loudness = one(*shards[0])
    for cut in shards[1:]:
        loudness = loudness * one(*cut)
    return loudness


def scatter_about(key, dims, spread, bound, cuts=(), kind=jnp.bfloat16):
    values = spread * jax.random.normal(key, dims, jnp.float32)
    if cuts:
        values = values * level_of(key, dims, cuts, -0.22, 0.18)
    return jnp.clip(values, -bound, bound).astype(kind)


def setup_inputs(seed: int = 0) -> dict:
    splits = jax.random.split(jax.random.key(seed), 8)
    return {
        "h_rows": scatter_about(splits[0], (N_GRID, NREG, NREG), 1.0, 6.0, ((0, 16), (1, 8))),
        "x_blocks": scatter_about(splits[1], (N_GRID, KB, NZ, BLK, BLK), (NZ * BLK) ** -0.5, 0.1875, ((0, 16), (1, 8))),
        "x_cols": with_ends(jax.random.randint(splits[2], (N_GRID, KB, NZ), 0, KB), jax.random.fold_in(splits[2], 1), 0, KB - 1).astype(jnp.int32),
        "sub_blocks": draw_sub_blocks(jax.random.fold_in(splits[7], 71), 0),
        "owners": draw_owners(jax.random.fold_in(splits[7], 71), 0),
        "shift_mu": jnp.clip(jax.random.uniform(splits[5], (1,), jnp.float32, -4.0, 4.0), -4.0, 4.0),
        "orbitals": scatter_about(splits[6], (N_ROW, N_GRID, OWN_MAX, ORDER, EXT), (16 * BLK) ** -0.5, 0.125, ((0, 8), (1, 16))),
    }


def densify(blocks, cols, count):
    onehot = (cols[:, :, None] == jnp.arange(count, dtype=jnp.int32)[None, None, :]).astype(jnp.float32)
    dense = jnp.einsum('rzk,rzab->rakb', onehot, blocks.astype(jnp.float32))
    return dense.reshape(blocks.shape[0] * blocks.shape[2], count * blocks.shape[2]).astype(jnp.bfloat16)

def sign_cols(mat, potential):
    eye = jnp.eye(ORDER, dtype=jnp.float32)
    shifted = mat.astype(jnp.float32) - potential * eye
    scale = jnp.sqrt(jnp.sum(shifted * shifted) / ORDER + 1e-06)
    first = (shifted / (2.0 * scale)).astype(jnp.bfloat16)
    square = jnp.dot(first, first, preferred_element_type=jnp.float32)
    helper = (3.0 * eye - square).astype(jnp.bfloat16)
    second = (0.5 * jnp.dot(first, helper, preferred_element_type=jnp.float32)).astype(jnp.bfloat16)
    square_cols = jnp.dot(second, second[:, :BLK], preferred_element_type=jnp.float32)
    helper_cols = (3.0 * eye[:, :BLK] - square_cols).astype(jnp.bfloat16)
    last = 0.5 * jnp.dot(second, helper_cols, preferred_element_type=jnp.float32)
    return (0.5 * (eye[:, :BLK] - last)).astype(jnp.bfloat16)

def extract(blocks4, picks):
    rows = jnp.take(blocks4, picks, axis=0)
    both = jnp.take(rows, picks, axis=2)
    return both.reshape(ORDER, ORDER)

def reference(h_rows, x_blocks, x_cols, sub_blocks, owners, shift_mu, orbitals):
    potential = shift_mu[0]
    count = x_cols.shape[1]
    subs_by_region = jnp.transpose(sub_blocks, (1, 0, 2, 3))

    def region(item):
        hmat, blocks, cols, picks = item
        dense = densify(blocks, cols, count)
        prod = jnp.dot(dense, hmat, preferred_element_type=jnp.float32).astype(jnp.bfloat16)
        blocks4 = prod.reshape(count, BLK, count, BLK)
        flat = picks.reshape(-1, SUB_BLK)
        result = lax.map(lambda p: sign_cols(extract(blocks4, p), potential), flat)
        return result.reshape(picks.shape[0], picks.shape[1], ORDER, BLK)
    dcols = lax.map(region, (h_rows, x_blocks, x_cols, subs_by_region))
    ngrid = h_rows.shape[0]
    nrow = sub_blocks.shape[0]
    nsub = owners.shape[2]
    pairs_r = jnp.repeat(jnp.arange(nrow, dtype=jnp.int32), ngrid)
    pairs_o = jnp.tile(jnp.arange(ngrid, dtype=jnp.int32), nrow)

    def collocate(item):
        rindex, oindex = item
        table = owners[rindex]
        hit = table == oindex
        has = jnp.any(hit, axis=1)
        which = lax.optimization_barrier(jnp.sum(jnp.arange(nsub, dtype=jnp.int32)[None, :] * hit.astype(jnp.int32), axis=1))
        place = jnp.cumsum(has.astype(jnp.int32)) - 1
        select = has[None, :] & (place[None, :] == jnp.arange(OWN_MAX, dtype=jnp.int32)[:, None])
        selint = select.astype(jnp.int32)
        source = lax.optimization_barrier(jnp.sum(selint * jnp.arange(ngrid, dtype=jnp.int32)[None, :], axis=1))
        slot_k = lax.optimization_barrier(jnp.sum(selint * which[None, :], axis=1))
        live = jnp.any(select, axis=1)
        cols = dcols[source, rindex, slot_k]
        phi = orbitals[rindex, oindex].astype(jnp.float32)
        proj = jnp.einsum('tnm,tnx->tmx', cols.astype(jnp.float32), phi)
        values = lax.optimization_barrier(jnp.sum(proj * phi[:, :BLK, :], axis=1))
        return lax.optimization_barrier(jnp.sum(jnp.where(live[:, None], values, 0.0), axis=0))
    windows = lax.map(collocate, (pairs_r, pairs_o)).reshape(nrow, ngrid, EXT)
    total = lax.optimization_barrier(jnp.sum(windows, axis=0)).reshape(ngrid, DEPTH + 2 * MARG, PLANE)
    core = total[:, MARG:MARG + DEPTH]
    lower = total[:, :MARG]
    upper = total[:, MARG + DEPTH:]
    core = core.at[:, :MARG].add(jnp.roll(upper, 1, axis=0))
    core = core.at[:, DEPTH - MARG:].add(jnp.roll(lower, -1, axis=0))
    return core.reshape(ngrid, CELLS)
```

```python
import jax
import jax.numpy as jnp
from jax import lax
from jax.experimental import pallas as pl
from jax.experimental.pallas import tpu as pltpu
from jax.sharding import PartitionSpec as P

BLK = 128
SUB_BLK = 6
NZ = 8
SUB_DEV = 3
OWN_MAX = 6
PLANE = 256
DEPTH = 4
MARG = 1
ORDER = 768
KB = 16
NREG = 2048
HALF = 8

X_DN, X_UP, X_SIB, X_FAR_A, X_FAR_B, X_SDN, X_SUP, X_SFAR_A, X_SFAR_B = range(9)
T_DN, T_UP, T_SIB, T_FAR, T_SDN, T_SUP, T_SFAR = range(9, 16)
H_DN, H_UP, H_SIB, H_FAR, H_SDN, H_SUP, H_SFAR = range(16, 30, 2)
N_SEM = 30


def eye_like(rows, cols, first_row):
    row = lax.broadcasted_iota(jnp.int32, (rows, cols), 0) + first_row
    col = lax.broadcasted_iota(jnp.int32, (rows, cols), 1)
    return row == col


def region_kernel(
    h_in, x_in, inv_in, same_in, picks, mu_in, out,
    h_own, h_dn, h_up, h_far, x_all, table, table_s, lhs, rhs, total, z0, y0, z1, y1,
    send_sem, recv_sem, own_sem, table_sem,
):
    r = lax.axis_index("row")
    g = lax.axis_index("grid")
    y = r // 2
    core = r - 2 * y
    sib = 2 * y + 1 - core
    y_up, y_dn, y_far = lax.rem(y + 1, 4), lax.rem(y + 3, 4), lax.rem(y + 2, 4)
    up, dn = 2 * y_up + core, 2 * y_dn + core

    barrier = pltpu.get_barrier_semaphore()
    for other in (up, dn, sib):
        pl.semaphore_signal(
            barrier, inc=1, device_id=(other, g), device_id_type=pl.DeviceIdType.MESH
        )

    for b in range(KB):
        pltpu.make_async_copy(
            h_in.at[:, b * BLK : (b + 1) * BLK], h_own.at[core, b], own_sem
        ).start()
    for i in range(2):
        for z in range(NZ):
            block = x_in[i, z].astype(jnp.float32)
            for w in range(z + 1, NZ):
                block += x_in[i, w].astype(jnp.float32) * same_in[(i * NZ + z) * NZ + w]
            x_all[2 * r + i, z] = block.astype(jnp.bfloat16)
    for i in range(KB):
        x_all[i, NZ] = jnp.zeros((BLK, BLK), jnp.bfloat16)
    table[pl.ds(2 * r, 2)] = inv_in[...]
    pl.semaphore_wait(barrier, 3)

    copies = {}

    def send(slot, src, dst, device):
        copy = pltpu.make_async_remote_copy(
            src_ref=src, dst_ref=dst, send_sem=send_sem.at[slot], recv_sem=recv_sem.at[slot],
            device_id=(device, g), device_id_type=pl.DeviceIdType.MESH,
        )
        copy.start()
        copies[slot] = copy

    def x_rows(origin):
        return x_all.at[pl.ds(2 * origin, 2), pl.ds(0, NZ)]

    def x_row(origin, i):
        return x_all.at[2 * origin + i, pl.ds(0, NZ)]

    for slot, device in ((X_DN, up), (X_UP, dn), (X_SIB, sib)):
        send(slot, x_rows(r), x_rows(r), device)
    def t_rows(origin):
        return table.at[pl.ds(2 * origin, 2)]

    for slot, device in ((T_DN, up), (T_UP, dn), (T_SIB, sib)):
        send(slot, t_rows(r), t_rows(r), device)

    def half(ref, which):
        return ref.at[core, pl.ds(which * HALF, HALF)]

    def h_half(which):
        return half(h_own, which)

    pltpu.make_async_copy(h_own.at[core], h_own.at[core], own_sem).wait()
    send(H_DN, h_half(0), half(h_dn, 0), up)
    send(H_UP + 1, h_half(1), half(h_up, 1), dn)
    send(H_SIB, h_half(0), half(h_own, 0), sib)
    send(H_SIB + 1, h_half(1), half(h_own, 1), sib)
    send(H_DN + 1, h_half(1), half(h_dn, 1), up)
    send(H_UP, h_half(0), half(h_up, 0), dn)

    copies[X_DN].wait_recv()
    send(X_FAR_A, x_row(dn, 0), x_row(dn, 0), up)
    send(X_SDN, x_rows(dn), x_rows(dn), sib)
    copies[X_UP].wait_recv()
    send(X_FAR_B, x_row(up, 1), x_row(up, 1), dn)
    send(X_SUP, x_rows(up), x_rows(up), sib)
    far = 2 * y_far + core
    copies[T_DN].wait_recv()
    send(T_FAR, t_rows(dn), t_rows(dn), up)
    send(T_SDN, t_rows(dn), t_rows(dn), sib)
    copies[T_UP].wait_recv()
    send(T_SUP, t_rows(up), t_rows(up), sib)
    copies[X_FAR_A].wait_recv()
    send(X_SFAR_A, x_row(far, 0), x_row(far, 0), sib)
    copies[X_FAR_B].wait_recv()
    send(X_SFAR_B, x_row(far, 1), x_row(far, 1), sib)
    copies[T_FAR].wait_recv()
    send(T_SFAR, t_rows(far), t_rows(far), sib)

    copies[H_DN].wait_recv()
    send(H_FAR, half(h_dn, 0), half(h_far, 0), up)
    send(H_SDN, half(h_dn, 0), half(h_dn, 0), sib)
    copies[H_UP + 1].wait_recv()
    send(H_FAR + 1, half(h_up, 1), half(h_far, 1), dn)
    send(H_SUP + 1, half(h_up, 1), half(h_up, 1), sib)

    for slot in (X_SIB, X_SDN, X_SUP, X_SFAR_A, X_SFAR_B, T_SIB, T_SDN, T_SUP, T_SFAR):
        copies[slot].wait_recv()
    table_copy = pltpu.make_async_copy(table, table_s, table_sem)
    table_copy.start()
    table_copy.wait()

    def accumulate(h_ref, chip, first):
        def one(k, carry):
            for b in range(SUB_BLK):
                pick = picks[k * SUB_BLK + b]
                for j in range(4):
                    z = table_s[pick, 0, 4 * chip + j]
                    lhs[b * BLK : (b + 1) * BLK, j * BLK : (j + 1) * BLK] = x_all[pick, z]
                for c in range(2):
                    rhs[c * 2 * BLK : (c + 1) * 2 * BLK, b * BLK : (b + 1) * BLK] = h_ref[
                        c, pick
                    ]
            part = jnp.dot(lhs[...], rhs[...], preferred_element_type=jnp.float32)
            if first:
                total[k] = part
            else:
                total[k] += part
            return carry

        lax.fori_loop(0, SUB_DEV, one, 0)

    copies[H_SIB].wait_recv()
    copies[H_SIB + 1].wait_recv()
    accumulate(h_own, y, True)

    copies[H_DN + 1].wait_recv()
    send(H_SDN + 1, half(h_dn, 1), half(h_dn, 1), sib)
    copies[H_UP].wait_recv()
    send(H_SUP, half(h_up, 0), half(h_up, 0), sib)
    copies[H_SDN].wait_recv()
    copies[H_SDN + 1].wait_recv()
    accumulate(h_dn, y_dn, False)
    copies[H_SUP].wait_recv()
    copies[H_SUP + 1].wait_recv()
    accumulate(h_up, y_up, False)

    copies[H_FAR].wait_recv()
    send(H_SFAR, half(h_far, 0), half(h_far, 0), sib)
    copies[H_FAR + 1].wait_recv()
    send(H_SFAR + 1, half(h_far, 1), half(h_far, 1), sib)
    copies[H_SFAR].wait_recv()
    copies[H_SFAR + 1].wait_recv()
    accumulate(h_far, y_far, False)

    mu = mu_in[0]

    def sign(k, carry):
        mat = total[k].astype(jnp.bfloat16).astype(jnp.float32)
        shifted = mat - jnp.where(eye_like(ORDER, ORDER, 0), mu, 0.0)
        scale = jnp.sqrt(jnp.sum(shifted * shifted, axis=(0, 1), keepdims=True) / ORDER + 1e-06)
        z0[...] = (shifted * (0.5 / scale)).astype(jnp.bfloat16)
        for m in range(3):
            rows = pl.ds(m * 2 * BLK, 2 * BLK)
            square = jnp.dot(z0[rows, :], z0[...], preferred_element_type=jnp.float32)
            diag = jnp.where(eye_like(2 * BLK, ORDER, m * 2 * BLK), 3.0, 0.0)
            y0[rows, :] = (diag - square).astype(jnp.bfloat16)
        for m in range(3):
            rows = pl.ds(m * 2 * BLK, 2 * BLK)
            step = jnp.dot(z0[rows, :], y0[...], preferred_element_type=jnp.float32)
            z1[rows, :] = (0.5 * step).astype(jnp.bfloat16)
        square = jnp.dot(z1[...], z1[:, :BLK], preferred_element_type=jnp.float32)
        eye = eye_like(ORDER, BLK, 0)
        y1[...] = (jnp.where(eye, 3.0, 0.0) - square).astype(jnp.bfloat16)
        last = 0.5 * jnp.dot(z1[...], y1[...], preferred_element_type=jnp.float32)
        out[k] = (0.5 * (jnp.where(eye, 1.0, 0.0) - last)).astype(jnp.bfloat16)
        return carry

    lax.fori_loop(0, SUB_DEV, sign, 0)
    for copy in copies.values():
        copy.wait_send()


def region(h_rows, x_blocks, inverse, same, picks, mu):
    vmem = pl.BlockSpec(memory_space=pltpu.VMEM)
    smem = pl.BlockSpec(memory_space=pltpu.SMEM)
    h_buf = pltpu.VMEM((2, KB, 2 * BLK, BLK), jnp.bfloat16)
    square = pltpu.VMEM((ORDER, ORDER), jnp.bfloat16)
    return pl.pallas_call(
        region_kernel,
        out_shape=jax.ShapeDtypeStruct((SUB_DEV, ORDER, BLK), jnp.bfloat16),
        in_specs=[pl.BlockSpec(memory_space=pl.ANY), vmem, vmem, smem, smem, smem],
        out_specs=vmem,
        scratch_shapes=[
            h_buf, h_buf, h_buf, h_buf,
            pltpu.VMEM((KB, NZ + 1, BLK, BLK), jnp.bfloat16),
            pltpu.VMEM((KB, 8, BLK), jnp.int32),
            pltpu.SMEM((KB, 8, BLK), jnp.int32),
            pltpu.VMEM((ORDER, 4 * BLK), jnp.bfloat16),
            pltpu.VMEM((4 * BLK, ORDER), jnp.bfloat16),
            pltpu.VMEM((SUB_DEV, ORDER, ORDER), jnp.float32),
            square, square, square,
            pltpu.VMEM((ORDER, BLK), jnp.bfloat16),
            pltpu.SemaphoreType.DMA((N_SEM,)),
            pltpu.SemaphoreType.DMA((N_SEM,)),
            pltpu.SemaphoreType.DMA,
            pltpu.SemaphoreType.DMA,
        ],
        compiler_params=pltpu.CompilerParams(
            collective_id=0, has_side_effects=True, vmem_limit_bytes=56 << 20
        ),
        name="region",
    )(h_rows, x_blocks, inverse, same, picks, mu)


def from_behind(value, axis, steps):
    count = lax.axis_size(axis)
    pairs = [(source, (source + steps) % count) for source in range(count)]
    return lax.ppermute(value, axis, pairs)


def cut_along(value, dim, devices):
    before, after = (value.shape[:dim], value.shape[dim + 1 :])
    return jnp.moveaxis(value.reshape(*before, devices, -1, *after), dim, 0)


def sum_at_owner(value, axis, dim):
    parts = cut_along(value, dim, lax.axis_size(axis))
    arrived = lax.all_to_all(parts, axis, split_axis=0, concat_axis=0, tiled=True)
    return arrived.sum(axis=0)


def inverse_table(cols):
    found = cols[:, :, None] == jnp.arange(KB, dtype=jnp.int32)[None, None, :]
    first = jnp.min(jnp.where(found, jnp.arange(NZ, dtype=jnp.int32)[None, :, None], NZ), axis=1)
    return jnp.zeros((2, 8, BLK), jnp.int32).at[:, :, :KB].set(first[:, None, :])


def same_column(cols):
    return (cols[:, :, None] == cols[:, None, :]).astype(jnp.float32).reshape(-1)


def on_device(h_rows, x_blocks, x_cols, sub_blocks, owners, shift_mu, orbitals):
    built = region(
        h_rows[0], x_blocks[0], inverse_table(x_cols[0]), same_column(x_cols[0]),
        sub_blocks.reshape(-1), shift_mu,
    )
    ngrid = lax.axis_size("grid")
    myself = lax.axis_index("grid")
    table = owners[0]
    targets = lax.dynamic_index_in_dim(table, myself, 0, keepdims=False)
    hit = table == myself
    has = jnp.any(hit, axis=1)
    place = jnp.cumsum(has.astype(jnp.int32)) - 1
    select = has[None, :] & (place[None, :] == jnp.arange(OWN_MAX, dtype=jnp.int32)[:, None])
    selint = select.astype(jnp.int32)
    source = jnp.sum(selint * jnp.arange(ngrid, dtype=jnp.int32)[None, :], axis=1)
    live = jnp.any(select, axis=1)
    outgoing = jnp.zeros((ngrid, ORDER, BLK), jnp.bfloat16).at[targets].set(built)
    incoming = lax.all_to_all(outgoing, "grid", split_axis=0, concat_axis=0, tiled=True)
    columns = jnp.take(incoming, source, axis=0)
    phi = orbitals[0, 0]
    proj = jnp.einsum("tnm,tnx->tmx", columns, phi, preferred_element_type=jnp.float32)
    values = jnp.sum(proj * phi[:, :BLK, :].astype(jnp.float32), axis=1)
    window = jnp.sum(jnp.where(live[:, None], values, 0.0), axis=0).reshape(DEPTH + 2 * MARG, PLANE)
    core = window[MARG : MARG + DEPTH]
    from_prev = from_behind(window[MARG + DEPTH :], "grid", 1)
    from_next = from_behind(window[:MARG], "grid", -1)
    core = core.at[:MARG].add(from_prev)
    core = core.at[DEPTH - MARG :].add(from_next)
    return sum_at_owner(core.reshape(1, DEPTH * PLANE), "row", 1)


def solution(mesh):
    in_specs = (
        P("grid", "row", None),
        P("grid", "row", None, None, None),
        P("grid", "row", None),
        P("row", "grid", None, None),
        P("row", None, None),
        P(),
        P("row", "grid", None, None, None),
    )
    out_specs = P("grid", "row")
    return jax.shard_map(
        on_device, mesh=mesh, in_specs=in_specs, out_specs=out_specs, check_vma=False
    )
```

```python
import jax
import jax.numpy as jnp
from jax import lax
from jax.experimental import pallas as pl
from jax.experimental.pallas import tpu as pltpu
from jax.sharding import PartitionSpec as P

BLK = 128
SUB_BLK = 6
NZ = 8
SUB_DEV = 3
OWN_MAX = 6
PLANE = 256
DEPTH = 4
MARG = 1
ORDER = 768
KB = 16
NREG = 2048
HALF = 8
SPLIT = 384
EXT = 1536

X_DN, X_UP, X_SIB, X_FAR_A, X_FAR_B, X_SDN, X_SUP, X_SFAR_A, X_SFAR_B = range(9)
T_DN, T_UP, T_SIB, T_FAR, T_SDN, T_SUP, T_SFAR = range(9, 16)
H_DN, H_UP, H_SIB, H_FAR, H_SDN, H_SUP, H_SFAR = range(16, 30, 2)
N_SEM = 30


def eye_like(rows, cols, first_row):
    row = lax.broadcasted_iota(jnp.int32, (rows, cols), 0) + first_row
    col = lax.broadcasted_iota(jnp.int32, (rows, cols), 1)
    return row == col


def region_kernel(
    h_in, x_in, inv_in, same_in, picks, mu_in, which_in, slots_in, live_in, phi_in, out,
    h_own, h_dn, h_up, h_far, x_all, table, table_s, lhs, rhs, total, z0, y0, z1, y1,
    phi, line_x, line_z, pack_x, pack_z, pass_x, pass_z, got_x, got_z, pieces, sums,
    send_sem, recv_sem, own_sem, table_sem, phi_sem,
    line_send, line_recv, swap_send, swap_recv, sum_send, sum_recv,
):
    r = lax.axis_index("row")
    g = lax.axis_index("grid")
    gz = g // 4
    gx = g - 4 * gz
    y = r // 2
    core = r - 2 * y
    sib = 2 * y + 1 - core
    y_up, y_dn, y_far = lax.rem(y + 1, 4), lax.rem(y + 3, 4), lax.rem(y + 2, 4)
    up, dn = 2 * y_up + core, 2 * y_dn + core

    x_next = 4 * gz + lax.rem(gx + 1, 4)
    x_prev = 4 * gz + lax.rem(gx + 3, 4)
    z_next = 4 * lax.rem(gz + 1, 4) + gx
    z_prev = 4 * lax.rem(gz + 3, 4) + gx
    brick_next = lax.rem(g + 1, 16)
    brick_prev = lax.rem(g + 15, 16)

    sums[...] = jnp.zeros_like(sums)
    barrier = pltpu.get_barrier_semaphore()

    def greet(row, grid):
        pl.semaphore_signal(
            barrier, inc=1, device_id=(row, grid), device_id_type=pl.DeviceIdType.MESH
        )

    for step in range(1, 8):
        greet(lax.rem(r + step, 8), g)
    for other in (x_next, x_prev, z_next, z_prev):
        greet(r, other)

    @pl.when(r < 2)
    def _():
        for row in range(8):
            greet(row, brick_prev)

    @pl.when(r >= 6)
    def _():
        for row in range(8):
            greet(row, brick_next)

    phi_copy = pltpu.make_async_copy(phi_in, phi, phi_sem)
    phi_copy.start()
    for b in range(KB):
        pltpu.make_async_copy(
            h_in.at[:, b * BLK : (b + 1) * BLK], h_own.at[core, b], own_sem
        ).start()
    for i in range(2):
        for z in range(NZ):
            block = x_in[i, z].astype(jnp.float32)
            for w in range(z + 1, NZ):
                block += x_in[i, w].astype(jnp.float32) * same_in[(i * NZ + z) * NZ + w]
            x_all[2 * r + i, z] = block.astype(jnp.bfloat16)
    for i in range(KB):
        x_all[i, NZ] = jnp.zeros((BLK, BLK), jnp.bfloat16)
    table[pl.ds(2 * r, 2)] = inv_in[...]
    pl.semaphore_wait(barrier, 15)

    copies = {}

    def send(slot, src, dst, device):
        copy = pltpu.make_async_remote_copy(
            src_ref=src, dst_ref=dst, send_sem=send_sem.at[slot], recv_sem=recv_sem.at[slot],
            device_id=(device, g), device_id_type=pl.DeviceIdType.MESH,
        )
        copy.start()
        copies[slot] = copy

    def x_rows(origin):
        return x_all.at[pl.ds(2 * origin, 2), pl.ds(0, NZ)]

    def x_row(origin, i):
        return x_all.at[2 * origin + i, pl.ds(0, NZ)]

    for slot, device in ((X_DN, up), (X_UP, dn), (X_SIB, sib)):
        send(slot, x_rows(r), x_rows(r), device)
    def t_rows(origin):
        return table.at[pl.ds(2 * origin, 2)]

    for slot, device in ((T_DN, up), (T_UP, dn), (T_SIB, sib)):
        send(slot, t_rows(r), t_rows(r), device)

    def half(ref, which):
        return ref.at[core, pl.ds(which * HALF, HALF)]

    def h_half(which):
        return half(h_own, which)

    pltpu.make_async_copy(h_own.at[core], h_own.at[core], own_sem).wait()
    send(H_DN, h_half(0), half(h_dn, 0), up)
    send(H_UP + 1, h_half(1), half(h_up, 1), dn)
    send(H_SIB, h_half(0), half(h_own, 0), sib)
    send(H_SIB + 1, h_half(1), half(h_own, 1), sib)
    send(H_DN + 1, h_half(1), half(h_dn, 1), up)
    send(H_UP, h_half(0), half(h_up, 0), dn)

    copies[X_DN].wait_recv()
    send(X_FAR_A, x_row(dn, 0), x_row(dn, 0), up)
    send(X_SDN, x_rows(dn), x_rows(dn), sib)
    copies[X_UP].wait_recv()
    send(X_FAR_B, x_row(up, 1), x_row(up, 1), dn)
    send(X_SUP, x_rows(up), x_rows(up), sib)
    far = 2 * y_far + core
    copies[T_DN].wait_recv()
    send(T_FAR, t_rows(dn), t_rows(dn), up)
    send(T_SDN, t_rows(dn), t_rows(dn), sib)
    copies[T_UP].wait_recv()
    send(T_SUP, t_rows(up), t_rows(up), sib)
    copies[X_FAR_A].wait_recv()
    send(X_SFAR_A, x_row(far, 0), x_row(far, 0), sib)
    copies[X_FAR_B].wait_recv()
    send(X_SFAR_B, x_row(far, 1), x_row(far, 1), sib)
    copies[T_FAR].wait_recv()
    send(T_SFAR, t_rows(far), t_rows(far), sib)

    copies[H_DN].wait_recv()
    send(H_FAR, half(h_dn, 0), half(h_far, 0), up)
    send(H_SDN, half(h_dn, 0), half(h_dn, 0), sib)
    copies[H_UP + 1].wait_recv()
    send(H_FAR + 1, half(h_up, 1), half(h_far, 1), dn)
    send(H_SUP + 1, half(h_up, 1), half(h_up, 1), sib)

    for slot in (X_SIB, X_SDN, X_SUP, X_SFAR_A, X_SFAR_B, T_SIB, T_SDN, T_SUP, T_SFAR):
        copies[slot].wait_recv()
    table_copy = pltpu.make_async_copy(table, table_s, table_sem)
    table_copy.start()
    table_copy.wait()

    def accumulate(h_ref, chip, first):
        def one(k, carry):
            for b in range(SUB_BLK):
                pick = picks[k * SUB_BLK + b]
                for j in range(4):
                    z = table_s[pick, 0, 4 * chip + j]
                    lhs[b * BLK : (b + 1) * BLK, j * BLK : (j + 1) * BLK] = x_all[pick, z]
                for c in range(2):
                    rhs[c * 2 * BLK : (c + 1) * 2 * BLK, b * BLK : (b + 1) * BLK] = h_ref[
                        c, pick
                    ]
            part = jnp.dot(lhs[...], rhs[...], preferred_element_type=jnp.float32)
            if first:
                total[k] = part
            else:
                total[k] += part
            return carry

        lax.fori_loop(0, SUB_DEV, one, 0)

    copies[H_SIB].wait_recv()
    copies[H_SIB + 1].wait_recv()
    accumulate(h_own, y, True)

    copies[H_DN + 1].wait_recv()
    send(H_SDN + 1, half(h_dn, 1), half(h_dn, 1), sib)
    copies[H_UP].wait_recv()
    send(H_SUP, half(h_up, 0), half(h_up, 0), sib)
    copies[H_SDN].wait_recv()
    copies[H_SDN + 1].wait_recv()
    accumulate(h_dn, y_dn, False)
    copies[H_SUP].wait_recv()
    copies[H_SUP + 1].wait_recv()
    accumulate(h_up, y_up, False)

    copies[H_FAR].wait_recv()
    send(H_SFAR, half(h_far, 0), half(h_far, 0), sib)
    copies[H_FAR + 1].wait_recv()
    send(H_SFAR + 1, half(h_far, 1), half(h_far, 1), sib)
    copies[H_SFAR].wait_recv()
    copies[H_SFAR + 1].wait_recv()
    accumulate(h_far, y_far, False)

    mu = mu_in[0]

    def line_copy(way, k):
        line, me, before, after = (
            (line_x, gx, x_prev, x_next) if way < 4 else (line_z, gz, z_prev, z_next)
        )
        kind = way % 4
        source = lax.rem(me + (0, 0, 3, 1)[kind], 4)
        rows = (pl.ds(0, SPLIT), pl.ds(0, SPLIT), pl.ds(0, SPLIT // 2), pl.ds(SPLIT // 2, SPLIT // 2))
        part = line.at[source, k, rows[kind]]
        return pltpu.make_async_remote_copy(
            src_ref=part, dst_ref=part,
            send_sem=line_send.at[way, k], recv_sem=line_recv.at[way, k],
            device_id=(r, (after, before, after, before)[kind]),
            device_id_type=pl.DeviceIdType.MESH,
        )

    def pass_on(k):
        for first in (0, 4):
            line_copy(first, k).wait_recv()
            line_copy(first + 2, k).start()
            line_copy(first + 1, k).wait_recv()
            line_copy(first + 3, k).start()

    def sign(k, carry):
        mat = total[k].astype(jnp.bfloat16).astype(jnp.float32)
        shifted = mat - jnp.where(eye_like(ORDER, ORDER, 0), mu, 0.0)
        scale = jnp.sqrt(jnp.sum(shifted * shifted, axis=(0, 1), keepdims=True) / ORDER + 1e-06)
        z0[...] = (shifted * (0.5 / scale)).astype(jnp.bfloat16)
        for m in range(3):
            rows = pl.ds(m * 2 * BLK, 2 * BLK)
            square = jnp.dot(z0[rows, :], z0[...], preferred_element_type=jnp.float32)
            diag = jnp.where(eye_like(2 * BLK, ORDER, m * 2 * BLK), 3.0, 0.0)
            y0[rows, :] = (diag - square).astype(jnp.bfloat16)
        for m in range(3):
            rows = pl.ds(m * 2 * BLK, 2 * BLK)
            step = jnp.dot(z0[rows, :], y0[...], preferred_element_type=jnp.float32)
            z1[rows, :] = (0.5 * step).astype(jnp.bfloat16)
        square = jnp.dot(z1[...], z1[:, :BLK], preferred_element_type=jnp.float32)
        eye = eye_like(ORDER, BLK, 0)
        y1[...] = (jnp.where(eye, 3.0, 0.0) - square).astype(jnp.bfloat16)
        last = 0.5 * jnp.dot(z1[...], y1[...], preferred_element_type=jnp.float32)
        columns = (0.5 * (jnp.where(eye, 1.0, 0.0) - last)).astype(jnp.bfloat16)
        line_x[gx, k] = columns[:SPLIT]
        line_z[gz, k] = columns[SPLIT:]
        for way in (0, 1, 4, 5):
            line_copy(way, k).start()

        @pl.when(k > 0)
        def _():
            pass_on(k - 1)

        return carry

    lax.fori_loop(0, SUB_DEV, sign, 0)
    pass_on(SUB_DEV - 1)
    for k in range(SUB_DEV):
        for way in (2, 3, 6, 7):
            line_copy(way, k).wait_recv()

    for s in range(4):
        for step in (2, 1, 3):
            to_z = lax.rem(gz + step, 4)
            pack_x[step, s] = line_x[s, which_in[(4 * gz + s) * 16 + 4 * to_z + gx]]
            to_x = lax.rem(gx + step, 4)
            pack_z[step, s] = line_z[s, which_in[(4 * s + gx) * 16 + 4 * gz + to_x]]

    def swap(slot, src, dst, device):
        return pltpu.make_async_remote_copy(
            src_ref=src, dst_ref=dst,
            send_sem=swap_send.at[slot], recv_sem=swap_recv.at[slot],
            device_id=(r, device), device_id_type=pl.DeviceIdType.MESH,
        )

    def swaps(base, pack, passed, got, me, before, after):
        first, last = pl.ds(0, 2), pl.ds(2, 2)
        away = [
            swap(base, pack.at[2, first], passed.at[0], after),
            swap(base + 1, pack.at[2, last], passed.at[1], before),
            swap(base + 2, pack.at[1], got.at[me], after),
            swap(base + 3, pack.at[3], got.at[me], before),
        ]
        far = [
            swap(base + 4, passed.at[0], got.at[lax.rem(me + 3, 4), first], after),
            swap(base + 5, passed.at[1], got.at[lax.rem(me + 1, 4), last], before),
        ]
        return away, far

    away_x, far_x = swaps(0, pack_x, pass_x, got_x, gz, z_prev, z_next)
    away_z, far_z = swaps(6, pack_z, pass_z, got_z, gx, x_prev, x_next)
    for one in (*away_x, *away_z):
        one.start()
    for s in range(4):
        got_x[gz, s] = line_x[s, which_in[(4 * gz + s) * 16 + g]]
        got_z[gx, s] = line_z[s, which_in[(4 * s + gx) * 16 + g]]
    for i in range(2):
        for away, far in ((away_x, far_x), (away_z, far_z)):
            away[i].wait_recv()
            far[i].start()
    for one in (*away_x[2:], *away_z[2:], *far_x, *far_z):
        one.wait_recv()
    phi_copy.wait()

    across = (((0,), (0,)), ((), ()))

    def collocate(t, window):
        from_z, from_x = slots_in[2 * t], slots_in[2 * t + 1]
        top, low = got_x[from_z, from_x], got_z[from_x, from_z]
        proj = lax.dot_general(
            top, phi[t, :SPLIT], across, preferred_element_type=jnp.float32
        ) + lax.dot_general(low, phi[t, SPLIT:], across, preferred_element_type=jnp.float32)
        values = jnp.sum(proj * phi[t, :BLK].astype(jnp.float32), axis=0, keepdims=True)
        return window + values * live_in[t]

    window = lax.fori_loop(0, OWN_MAX, collocate, jnp.zeros((1, EXT), jnp.float32))
    for i in range(EXT // BLK):
        pieces[i] = window[:, i * BLK : (i + 1) * BLK]

    def give(slot, piece, place, row, grid):
        copy = pltpu.make_async_remote_copy(
            src_ref=pieces.at[piece], dst_ref=sums.at[place],
            send_sem=sum_send.at[slot], recv_sem=sum_recv.at[place],
            device_id=(row, grid), device_id_type=pl.DeviceIdType.MESH,
        )
        copy.start()
        return copy

    given = []
    for row in range(2):
        given.append(give(7 + row, 10 + row, 8 + r, row, brick_next))
        given.append(give(9 + row, row, 8 + r, 6 + row, brick_prev))
    for step in range(1, 8):
        row = lax.rem(r + step, 8)
        given.append(give(step - 1, 2 + row, r, row, g))
    sums[r] = pieces[2 + r]

    def arrived(place):
        pltpu.make_async_copy(sums.at[place], sums.at[place], sum_recv.at[place]).wait()

    for step in range(1, 8):
        arrived(lax.rem(r + step, 8))

    @pl.when((r < 2) | (r >= 6))
    def _():
        for row in range(8):
            arrived(8 + row)

    out[...] = jnp.sum(sums[...], axis=0)
    for copy in (*copies.values(), *away_x, *away_z, *far_x, *far_z, *given):
        copy.wait_send()
    for k in range(SUB_DEV):
        for way in range(8):
            line_copy(way, k).wait_send()


def region(h_rows, x_blocks, inverse, same, picks, mu, which, slots, live, orbitals):
    vmem = pl.BlockSpec(memory_space=pltpu.VMEM)
    smem = pl.BlockSpec(memory_space=pltpu.SMEM)
    hbm = pl.BlockSpec(memory_space=pl.ANY)
    h_buf = pltpu.VMEM((2, KB, 2 * BLK, BLK), jnp.bfloat16)
    square = pltpu.VMEM((ORDER, ORDER), jnp.bfloat16)
    line = pltpu.VMEM((4, SUB_DEV, SPLIT, BLK), jnp.bfloat16)
    slots4 = pltpu.VMEM((4, 4, SPLIT, BLK), jnp.bfloat16)
    slots2 = pltpu.VMEM((2, 2, SPLIT, BLK), jnp.bfloat16)
    dma = pltpu.SemaphoreType.DMA
    return pl.pallas_call(
        region_kernel,
        out_shape=jax.ShapeDtypeStruct((1, BLK), jnp.float32),
        in_specs=[hbm, vmem, vmem, smem, smem, smem, smem, smem, smem, hbm],
        out_specs=vmem,
        scratch_shapes=[
            h_buf, h_buf, h_buf, h_buf,
            pltpu.VMEM((KB, NZ + 1, BLK, BLK), jnp.bfloat16),
            pltpu.VMEM((KB, 8, BLK), jnp.int32),
            pltpu.SMEM((KB, 8, BLK), jnp.int32),
            pltpu.VMEM((ORDER, 4 * BLK), jnp.bfloat16),
            pltpu.VMEM((4 * BLK, ORDER), jnp.bfloat16),
            pltpu.VMEM((SUB_DEV, ORDER, ORDER), jnp.float32),
            square, square, square,
            pltpu.VMEM((ORDER, BLK), jnp.bfloat16),
            pltpu.VMEM((OWN_MAX, ORDER, EXT), jnp.bfloat16),
            line, line, slots4, slots4, slots2, slots2, slots4, slots4,
            pltpu.VMEM((EXT // BLK, 1, BLK), jnp.float32),
            pltpu.VMEM((16, 1, BLK), jnp.float32),
            dma((N_SEM,)), dma((N_SEM,)), dma, dma, dma,
            dma((8, SUB_DEV)), dma((8, SUB_DEV)), dma((12,)), dma((12,)), dma((11,)), dma((16,)),
        ],
        compiler_params=pltpu.CompilerParams(
            collective_id=0, has_side_effects=True, vmem_limit_bytes=60 << 20
        ),
        name="region",
    )(h_rows, x_blocks, inverse, same, picks, mu, which, slots, live, orbitals)


def inverse_table(cols):
    found = cols[:, :, None] == jnp.arange(KB, dtype=jnp.int32)[None, None, :]
    first = jnp.min(jnp.where(found, jnp.arange(NZ, dtype=jnp.int32)[None, :, None], NZ), axis=1)
    return jnp.zeros((2, 8, BLK), jnp.int32).at[:, :, :KB].set(first[:, None, :])


def same_column(cols):
    return (cols[:, :, None] == cols[:, None, :]).astype(jnp.float32).reshape(-1)


def on_device(h_rows, x_blocks, x_cols, sub_blocks, owners, shift_mu, orbitals):
    ngrid = lax.axis_size("grid")
    myself = lax.axis_index("grid")
    table = owners[0]
    bricks = jnp.arange(ngrid, dtype=jnp.int32)
    turn = jnp.arange(SUB_DEV, dtype=jnp.int32)
    which = jnp.sum(
        jnp.where(table[:, None, :] == bricks[None, :, None], turn[None, None, :], 0), axis=2
    )
    has = jnp.any(table == myself, axis=1)
    place = jnp.sum((has[None, :] & (bricks[None, :] < bricks[:, None])).astype(jnp.int32), axis=1)
    select = has[None, :] & (place[None, :] == jnp.arange(OWN_MAX, dtype=jnp.int32)[:, None])
    source = jnp.sum(jnp.where(select, bricks[None, :], 0), axis=1)
    live = jnp.any(select, axis=1).astype(jnp.float32)
    slots = jnp.stack([source // 4, source % 4], axis=1).reshape(-1)
    return region(
        h_rows[0], x_blocks[0], inverse_table(x_cols[0]), same_column(x_cols[0]),
        sub_blocks.reshape(-1), shift_mu, which.reshape(-1), slots, live, orbitals[0, 0],
    )


def solution(mesh):
    in_specs = (
        P("grid", "row", None),
        P("grid", "row", None, None, None),
        P("grid", "row", None),
        P("row", "grid", None, None),
        P("row", None, None),
        P(),
        P("row", "grid", None, None, None),
    )
    out_specs = P("grid", "row")
    return jax.shard_map(
        on_device, mesh=mesh, in_specs=in_specs, out_specs=out_specs, check_vma=False
    )
```

```python
import jax
import jax.numpy as jnp
from jax import lax
from jax.experimental import pallas as pl
from jax.experimental.pallas import tpu as pltpu
from jax.sharding import PartitionSpec as P

BLK = 128
SUB_BLK = 6
NZ = 8
SUB_DEV = 3
OWN_MAX = 6
PLANE = 256
DEPTH = 4
MARG = 1
ORDER = 768
KB = 16
NREG = 2048
HALF = 64
TILE = 256
SPLIT = 384
EXT = 1536

X_DN, X_UP, X_SIB, X_FAR_A, X_FAR_B, X_SDN, X_SUP, X_SFAR_A, X_SFAR_B = range(9)
T_DN, T_UP, T_SIB, T_FAR, T_SDN, T_SUP, T_SFAR = range(9, 16)
H_DN, H_UP, H_SIB, H_SDN, H_SUP, H_FAR_A, H_FAR_B, H_SFAR_A, H_SFAR_B = range(16, 34, 2)
N_SEM = 34


def eye_like(rows, cols, first_row):
    row = lax.broadcasted_iota(jnp.int32, (rows, cols), 0) + first_row
    col = lax.broadcasted_iota(jnp.int32, (rows, cols), 1)
    return row == col


def region_kernel(
    h_in, x_in, cols_in, picks, owners, mu_in, phi_in, out,
    h_own, h_dn, h_up, h_far_a, h_far_b, x_all, table, table_s, lhs, rhs, total, w, y0, z1, y1,
    phi, line_x, line_z, pack_x, pack_z, pass_x, pass_z, got_x, got_z, column, pieces, sums,
    send_sem, recv_sem, own_sem, table_sem, phi_sem,
    line_send, line_recv, swap_send, swap_recv, sum_send, sum_recv,
):
    r = lax.axis_index("row")
    g = lax.axis_index("grid")
    gz = g // 4
    gx = g - 4 * gz
    y = r // 2
    core = r - 2 * y
    sib = 2 * y + 1 - core
    y_up, y_dn, y_far = lax.rem(y + 1, 4), lax.rem(y + 3, 4), lax.rem(y + 2, 4)
    up, dn = 2 * y_up + core, 2 * y_dn + core
    x_next = 4 * gz + lax.rem(gx + 1, 4)
    x_prev = 4 * gz + lax.rem(gx + 3, 4)
    z_next = 4 * lax.rem(gz + 1, 4) + gx
    z_prev = 4 * lax.rem(gz + 3, 4) + gx
    brick_next = lax.rem(g + 1, 16)
    brick_prev = lax.rem(g + 15, 16)

    for b in range(KB):
        pltpu.make_async_copy(
            h_in.at[:, b * BLK : (b + 1) * BLK], h_own.at[core, b], own_sem
        ).start()
    sums[...] = jnp.zeros_like(sums)
    barrier = pltpu.get_barrier_semaphore()

    def greet(row, grid):
        pl.semaphore_signal(
            barrier, inc=1, device_id=(row, grid), device_id_type=pl.DeviceIdType.MESH
        )

    for step in range(1, 8):
        greet(lax.rem(r + step, 8), g)
    for other in (x_next, x_prev, z_next, z_prev):
        greet(r, other)

    @pl.when(r < 2)
    def _():
        for row in range(8):
            greet(row, brick_prev)

    @pl.when(r >= 6)
    def _():
        for row in range(8):
            greet(row, brick_next)

    copies = {}

    def send(slot, src, dst, device):
        copy = pltpu.make_async_remote_copy(
            src_ref=src, dst_ref=dst, send_sem=send_sem.at[slot], recv_sem=recv_sem.at[slot],
            device_id=(device, g), device_id_type=pl.DeviceIdType.MESH,
        )
        copy.start()
        copies[slot] = copy

    def half(ref, which):
        return ref.at[core, pl.ds(0, KB), pl.ds(which * BLK, BLK)]

    def far_part(ref, which):
        return ref.at[core, pl.ds(0, KB), pl.ds(which * HALF, HALF)]

    def near_part(ref, block, which):
        return ref.at[core, pl.ds(0, KB), pl.ds(block * BLK + which * HALF, HALF)]

    def x_rows(origin):
        return x_all.at[pl.ds(2 * origin, 2), pl.ds(0, NZ)]

    def x_row(origin, i):
        return x_all.at[2 * origin + i, pl.ds(0, NZ)]

    def t_rows(origin):
        return table.at[pl.ds(2 * origin, 2)]

    pltpu.make_async_copy(h_own.at[core], h_own.at[core], own_sem).wait()
    pl.semaphore_wait(barrier, 15)
    for slot, ref, device in ((H_DN, h_dn, up), (H_UP, h_up, dn), (H_SIB, h_own, sib)):
        send(slot, half(h_own, 0), half(ref, 0), device)

    lane = lax.broadcasted_iota(jnp.int32, (8, BLK), 1)
    for i in range(2):
        first = jnp.full((8, BLK), NZ, jnp.int32)
        for z in reversed(range(NZ)):
            first = jnp.where(lane == cols_in[i, z], z, first)
        table[2 * r + i] = first
        for z in range(NZ):
            block = x_in[i, z].astype(jnp.float32)
            for v in range(z + 1, NZ):
                same = (cols_in[i, v] == cols_in[i, z]).astype(jnp.int32).astype(jnp.float32)
                block += x_in[i, v].astype(jnp.float32) * same
            x_all[2 * r + i, z] = block.astype(jnp.bfloat16)
    for slot, device in ((X_DN, up), (X_UP, dn), (X_SIB, sib)):
        send(slot, x_rows(r), x_rows(r), device)
    for slot, device in ((T_DN, up), (T_UP, dn), (T_SIB, sib)):
        send(slot, t_rows(r), t_rows(r), device)
    for slot, ref, device in ((H_DN, h_dn, up), (H_UP, h_up, dn), (H_SIB, h_own, sib)):
        send(slot + 1, half(h_own, 1), half(ref, 1), device)
    phi_copy = pltpu.make_async_copy(phi_in, phi, phi_sem)
    phi_copy.start()
    for i in range(KB):
        x_all[i, NZ] = jnp.zeros((BLK, BLK), jnp.bfloat16)

    def item_for(source, owner):
        found = sum(k * (owners[source, k] == owner).astype(jnp.int32) for k in range(1, SUB_DEV))
        return jnp.minimum(found, SUB_DEV - 1)

    count = jnp.int32(0)
    slot_source = [jnp.int32(0)] * OWN_MAX
    for source in range(16):
        has = sum((owners[source, k] == g).astype(jnp.int32) for k in range(SUB_DEV))
        has = jnp.minimum(has, 1)
        for t in range(OWN_MAX):
            slot_source[t] += source * has * (count == t).astype(jnp.int32)
        count += has

    def relay_h(block):
        far, far_ref = (H_FAR_A, h_far_a) if block == 0 else (H_FAR_B, h_far_b)
        copies[H_DN + block].wait_recv()
        send(far, near_part(h_dn, block, 0), far_part(far_ref, 0), up)
        send(H_SDN + block, half(h_dn, block), half(h_dn, block), sib)
        copies[H_UP + block].wait_recv()
        send(far + 1, near_part(h_up, block, 1), far_part(far_ref, 1), dn)
        send(H_SUP + block, half(h_up, block), half(h_up, block), sib)

    far = 2 * y_far + core
    copies[X_DN].wait_recv()
    send(X_FAR_A, x_row(dn, 0), x_row(dn, 0), up)
    send(X_SDN, x_rows(dn), x_rows(dn), sib)
    copies[X_UP].wait_recv()
    send(X_FAR_B, x_row(up, 1), x_row(up, 1), dn)
    send(X_SUP, x_rows(up), x_rows(up), sib)
    copies[T_DN].wait_recv()
    send(T_FAR, t_rows(dn), t_rows(dn), up)
    send(T_SDN, t_rows(dn), t_rows(dn), sib)
    copies[T_UP].wait_recv()
    send(T_SUP, t_rows(up), t_rows(up), sib)
    relay_h(0)
    copies[X_FAR_A].wait_recv()
    send(X_SFAR_A, x_row(far, 0), x_row(far, 0), sib)
    copies[X_FAR_B].wait_recv()
    send(X_SFAR_B, x_row(far, 1), x_row(far, 1), sib)
    copies[T_FAR].wait_recv()
    send(T_SFAR, t_rows(far), t_rows(far), sib)

    for slot in (X_SIB, X_SDN, X_SUP, X_SFAR_A, X_SFAR_B, T_SIB, T_SDN, T_SUP, T_SFAR):
        copies[slot].wait_recv()
    table_copy = pltpu.make_async_copy(table, table_s, table_sem)
    table_copy.start()
    table_copy.wait()

    def pick_blocks(k, h_ref, chip, blocks):
        for b in range(SUB_BLK):
            pick = picks[k, b]
            rows = slice(b * BLK, (b + 1) * BLK)
            for c in range(2):
                for n, block in enumerate(blocks):
                    z = table_s[pick, 0, 4 * chip + 2 * c + block]
                    at = (c * len(blocks) + n) * BLK
                    lhs[rows, at : at + BLK] = x_all[pick, z]
                depth = len(blocks) * BLK
                rhs[c * depth : (c + 1) * depth, rows] = h_ref[c, pick]

    def accumulate(h_ref, chip, blocks, first):
        depth = 2 * len(blocks) * BLK

        def one(k, carry):
            pick_blocks(k, h_ref, chip, blocks)
            part = jnp.dot(lhs[:, :depth], rhs[:depth, :], preferred_element_type=jnp.float32)
            if first:
                total[k] = part
            else:
                total[k] += part
            return carry

        lax.fori_loop(0, SUB_DEV, one, 0)

    copies[H_SIB].wait_recv()
    copies[H_SIB + 1].wait_recv()
    accumulate(h_own, y, (0, 1), True)
    relay_h(1)
    for ref, slot, chip in ((h_dn, H_SDN, y_dn), (h_up, H_SUP, y_up)):
        copies[slot].wait_recv()
        copies[slot + 1].wait_recv()
        accumulate(ref, chip, (0, 1), False)
    for far, passed, ref in ((H_FAR_A, H_SFAR_A, h_far_a), (H_FAR_B, H_SFAR_B, h_far_b)):
        for which in range(2):
            copies[far + which].wait_recv()
            send(passed + which, far_part(ref, which), far_part(ref, which), sib)
        for which in range(2):
            copies[passed + which].wait_recv()
        if far == H_FAR_A:
            accumulate(ref, y_far, (0,), False)

    mu = mu_in[0]

    def line_copy(way, k):
        line, me, before, after = (
            (line_x, gx, x_prev, x_next) if way < 4 else (line_z, gz, z_prev, z_next)
        )
        kind = way % 4
        source = lax.rem(me + (0, 0, 3, 1)[kind], 4)
        rows = (pl.ds(0, SPLIT), pl.ds(0, SPLIT), pl.ds(0, SPLIT // 2), pl.ds(SPLIT // 2, SPLIT // 2))
        part = line.at[source, k, rows[kind]]
        return pltpu.make_async_remote_copy(
            src_ref=part, dst_ref=part,
            send_sem=line_send.at[way, k], recv_sem=line_recv.at[way, k],
            device_id=(r, (after, before, after, before)[kind]),
            device_id_type=pl.DeviceIdType.MESH,
        )

    def pass_on(k):
        for first in (0, 4):
            line_copy(first, k).wait_recv()
            line_copy(first + 2, k).start()
            line_copy(first + 1, k).wait_recv()
            line_copy(first + 3, k).start()

    def sign(k, carry):
        pick_blocks(k, h_far_b, y_far, (1,))
        norm = jnp.zeros((1, TILE), jnp.float32)
        for n in range(3):
            cols = slice(n * TILE, (n + 1) * TILE)
            part = jnp.dot(
                lhs[:, :TILE], rhs[:TILE, cols], preferred_element_type=jnp.float32
            )
            mat = (total[k, :, cols] + part).astype(jnp.bfloat16).astype(jnp.float32)
            shifted = mat - jnp.where(eye_like(ORDER, TILE, -n * TILE), mu, 0.0)
            norm += jnp.sum(shifted * shifted, axis=0, keepdims=True)
            w[:, cols] = shifted.astype(jnp.bfloat16)
        square_scale = jnp.sum(norm, axis=1, keepdims=True) / ORDER + 1e-06
        scale_y = 0.25 / square_scale
        scale_z = 0.25 / jnp.sqrt(square_scale)
        for n in range(3):
            cols = slice(n * TILE, (n + 1) * TILE)
            square = jnp.dot(w[...], w[:, cols], preferred_element_type=jnp.float32)
            diag = jnp.where(eye_like(ORDER, TILE, -n * TILE), 3.0, 0.0)
            y0[:, cols] = (diag - scale_y * square).astype(jnp.bfloat16)
        for n in range(3):
            cols = slice(n * TILE, (n + 1) * TILE)
            step = jnp.dot(w[...], y0[:, cols], preferred_element_type=jnp.float32)
            z1[:, cols] = (scale_z * step).astype(jnp.bfloat16)
        square = jnp.dot(z1[...], z1[:, :BLK], preferred_element_type=jnp.float32)
        eye = eye_like(ORDER, BLK, 0)
        y1[...] = (jnp.where(eye, 3.0, 0.0) - square).astype(jnp.bfloat16)
        last = 0.5 * jnp.dot(z1[...], y1[...], preferred_element_type=jnp.float32)
        columns = (0.5 * (jnp.where(eye, 1.0, 0.0) - last)).astype(jnp.bfloat16)
        line_x[gx, k] = columns[:SPLIT]
        line_z[gz, k] = columns[SPLIT:]
        for way in (0, 1, 4, 5):
            line_copy(way, k).start()

        @pl.when(k > 0)
        def _():
            pass_on(k - 1)

        return carry

    lax.fori_loop(0, SUB_DEV, sign, 0)
    pass_on(SUB_DEV - 1)
    for k in range(SUB_DEV):
        for way in (2, 3, 6, 7):
            line_copy(way, k).wait_recv()

    for s in range(4):
        for step in (2, 1, 3):
            to_z = lax.rem(gz + step, 4)
            pack_x[step, s] = line_x[s, item_for(4 * gz + s, 4 * to_z + gx)]
            to_x = lax.rem(gx + step, 4)
            pack_z[step, s] = line_z[s, item_for(4 * s + gx, 4 * gz + to_x)]

    def swap(slot, src, dst, device):
        return pltpu.make_async_remote_copy(
            src_ref=src, dst_ref=dst,
            send_sem=swap_send.at[slot], recv_sem=swap_recv.at[slot],
            device_id=(r, device), device_id_type=pl.DeviceIdType.MESH,
        )

    def swaps(base, pack, passed, got, me, before, after):
        first, last = pl.ds(0, 2), pl.ds(2, 2)
        away = [
            swap(base, pack.at[2, first], passed.at[0], after),
            swap(base + 1, pack.at[2, last], passed.at[1], before),
            swap(base + 2, pack.at[1], got.at[me], after),
            swap(base + 3, pack.at[3], got.at[me], before),
        ]
        far = [
            swap(base + 4, passed.at[0], got.at[lax.rem(me + 3, 4), first], after),
            swap(base + 5, passed.at[1], got.at[lax.rem(me + 1, 4), last], before),
        ]
        return away, far

    away_x, far_x = swaps(0, pack_x, pass_x, got_x, gz, z_prev, z_next)
    away_z, far_z = swaps(6, pack_z, pass_z, got_z, gx, x_prev, x_next)
    for one in (*away_x, *away_z):
        one.start()
    for s in range(4):
        got_x[gz, s] = line_x[s, item_for(4 * gz + s, g)]
        got_z[gx, s] = line_z[s, item_for(4 * s + gx, g)]
    for i in range(2):
        for away, far in ((away_x, far_x), (away_z, far_z)):
            away[i].wait_recv()
            far[i].start()
    for one in (*away_x[2:], *away_z[2:], *far_x, *far_z):
        one.wait_recv()
    phi_copy.wait()

    across = (((0,), (0,)), ((), ()))
    window = jnp.zeros((1, EXT), jnp.float32)
    for t in range(OWN_MAX):
        from_z = slot_source[t] // 4
        from_x = slot_source[t] - 4 * from_z
        column[:SPLIT] = got_x[from_z, from_x]
        column[SPLIT:] = got_z[from_x, from_z]
        proj = lax.dot_general(column[...], phi[t], across, preferred_element_type=jnp.float32)
        values = jnp.sum(proj * phi[t, :BLK].astype(jnp.float32), axis=0, keepdims=True)
        window += values * (count > t).astype(jnp.int32).astype(jnp.float32)
    for i in range(EXT // BLK):
        pieces[i] = window[:, i * BLK : (i + 1) * BLK]

    def give(slot, piece, place, row, grid):
        copy = pltpu.make_async_remote_copy(
            src_ref=pieces.at[piece], dst_ref=sums.at[place],
            send_sem=sum_send.at[slot], recv_sem=sum_recv.at[place],
            device_id=(row, grid), device_id_type=pl.DeviceIdType.MESH,
        )
        copy.start()
        return copy

    given = []
    for row in range(2):
        given.append(give(7 + row, 10 + row, 8 + r, row, brick_next))
        given.append(give(9 + row, row, 8 + r, 6 + row, brick_prev))
    for step in range(1, 8):
        row = lax.rem(r + step, 8)
        given.append(give(step - 1, 2 + row, r, row, g))
    sums[r] = pieces[2 + r]

    def arrived(place):
        pltpu.make_async_copy(sums.at[place], sums.at[place], sum_recv.at[place]).wait()

    for step in range(1, 8):
        arrived(lax.rem(r + step, 8))

    @pl.when((r < 2) | (r >= 6))
    def _():
        for row in range(8):
            arrived(8 + row)

    out[...] = jnp.sum(sums[...], axis=0)
    for copy in (*copies.values(), *away_x, *away_z, *far_x, *far_z, *given):
        copy.wait_send()
    for k in range(SUB_DEV):
        for way in range(8):
            line_copy(way, k).wait_send()


def region(h_rows, x_blocks, x_cols, picks, owners, mu, orbitals):
    vmem = pl.BlockSpec(memory_space=pltpu.VMEM)
    smem = pl.BlockSpec(memory_space=pltpu.SMEM)
    hbm = pl.BlockSpec(memory_space=pl.ANY)
    h_buf = pltpu.VMEM((2, KB, 2 * BLK, BLK), jnp.bfloat16)
    h_far = pltpu.VMEM((2, KB, BLK, BLK), jnp.bfloat16)
    square = pltpu.VMEM((ORDER, ORDER), jnp.bfloat16)
    columns = pltpu.VMEM((ORDER, BLK), jnp.bfloat16)
    line = pltpu.VMEM((4, SUB_DEV, SPLIT, BLK), jnp.bfloat16)
    slots4 = pltpu.VMEM((4, 4, SPLIT, BLK), jnp.bfloat16)
    slots2 = pltpu.VMEM((2, 2, SPLIT, BLK), jnp.bfloat16)
    dma = pltpu.SemaphoreType.DMA
    return pl.pallas_call(
        region_kernel,
        out_shape=jax.ShapeDtypeStruct((1, BLK), jnp.float32),
        in_specs=[hbm, vmem, smem, smem, smem, smem, hbm],
        out_specs=vmem,
        scratch_shapes=[
            h_buf, h_buf, h_buf, h_far, h_far,
            pltpu.VMEM((KB, NZ + 1, BLK, BLK), jnp.bfloat16),
            pltpu.VMEM((KB, 8, BLK), jnp.int32),
            pltpu.SMEM((KB, 8, BLK), jnp.int32),
            pltpu.VMEM((ORDER, 4 * BLK), jnp.bfloat16),
            pltpu.VMEM((4 * BLK, ORDER), jnp.bfloat16),
            pltpu.VMEM((SUB_DEV, ORDER, ORDER), jnp.float32),
            square, square, square, columns,
            pltpu.VMEM((OWN_MAX, ORDER, EXT), jnp.bfloat16),
            line, line, slots4, slots4, slots2, slots2, slots4, slots4, columns,
            pltpu.VMEM((EXT // BLK, 1, BLK), jnp.float32),
            pltpu.VMEM((16, 1, BLK), jnp.float32),
            dma((N_SEM,)), dma((N_SEM,)), dma, dma, dma,
            dma((8, SUB_DEV)), dma((8, SUB_DEV)), dma((12,)), dma((12,)), dma((11,)), dma((16,)),
        ],
        compiler_params=pltpu.CompilerParams(
            collective_id=0, has_side_effects=True, vmem_limit_bytes=60 << 20
        ),
        name="region",
    )(h_rows, x_blocks, x_cols, picks, owners, mu, orbitals)


def on_device(h_rows, x_blocks, x_cols, sub_blocks, owners, shift_mu, orbitals):
    return region(
        h_rows[0], x_blocks[0], x_cols[0], sub_blocks[0, 0], owners[0], shift_mu, orbitals[0, 0]
    )


def solution(mesh):
    in_specs = (
        P("grid", "row", None),
        P("grid", "row", None, None, None),
        P("grid", "row", None),
        P("row", "grid", None, None),
        P("row", None, None),
        P(),
        P("row", "grid", None, None, None),
    )
    out_specs = P("grid", "row")
    return jax.shard_map(
        on_device, mesh=mesh, in_specs=in_specs, out_specs=out_specs, check_vma=False
    )
```

```python
import jax
import jax.numpy as jnp
from jax import lax
from jax.experimental import pallas as pl
from jax.experimental.pallas import tpu as pltpu
from jax.sharding import PartitionSpec as P

BLK = 128
SUB_BLK = 6
NZ = 8
SUB_DEV = 3
OWN_MAX = 6
PLANE = 256
DEPTH = 4
MARG = 1
ORDER = 768
KB = 16
NREG = 2048
HALF = 64
TILE = 256
SPLIT = 384
EXT = 1536

X_DN, X_UP, X_SIB, X_FAR_A, X_FAR_B, X_SDN, X_SUP, X_SFAR_A, X_SFAR_B = range(9)
T_DN, T_UP, T_SIB, T_FAR, T_SDN, T_SUP, T_SFAR = range(9, 16)
H_DN, H_UP, H_SIB, H_SDN, H_SUP, H_FAR_A, H_FAR_B, H_SFAR_A, H_SFAR_B = range(16, 34, 2)
N_SEM = 34


def eye_like(rows, cols, first_row):
    row = lax.broadcasted_iota(jnp.int32, (rows, cols), 0) + first_row
    col = lax.broadcasted_iota(jnp.int32, (rows, cols), 1)
    return row == col


def region_kernel(
    h_in, x_in, cols_in, picks, owners, mu_in, phi_in, out,
    h_own, h_dn, h_up, h_far_a, h_far_b, x_all, table, table_s, lhs, rhs, total, w, y0, z1, y1,
    phi, line_x, line_z, pack_x, pack_z, pass_x, pass_z, got_x, got_z, column, pieces, sums,
    send_sem, recv_sem, own_sem, table_sem, phi_sem,
    line_send, line_recv, swap_send, swap_recv, sum_send, sum_recv,
):
    r = lax.axis_index("row")
    g = lax.axis_index("grid")
    gz = g // 4
    gx = g - 4 * gz
    y = r // 2
    core = r - 2 * y
    sib = 2 * y + 1 - core
    y_up, y_dn, y_far = lax.rem(y + 1, 4), lax.rem(y + 3, 4), lax.rem(y + 2, 4)
    up, dn = 2 * y_up + core, 2 * y_dn + core
    x_next = 4 * gz + lax.rem(gx + 1, 4)
    x_prev = 4 * gz + lax.rem(gx + 3, 4)
    z_next = 4 * lax.rem(gz + 1, 4) + gx
    z_prev = 4 * lax.rem(gz + 3, 4) + gx
    brick_next = lax.rem(g + 1, 16)
    brick_prev = lax.rem(g + 15, 16)

    for b in range(KB):
        pltpu.make_async_copy(
            h_in.at[:, b * BLK : (b + 1) * BLK], h_own.at[core, b], own_sem
        ).start()
    sums[...] = jnp.zeros_like(sums)
    barrier = pltpu.get_barrier_semaphore()

    def greet(row, grid):
        pl.semaphore_signal(
            barrier, inc=1, device_id=(row, grid), device_id_type=pl.DeviceIdType.MESH
        )

    for step in range(1, 8):
        greet(lax.rem(r + step, 8), g)
    for other in (x_next, x_prev, z_next, z_prev):
        greet(r, other)

    @pl.when(r < 2)
    def _():
        for row in range(8):
            greet(row, brick_prev)

    @pl.when(r >= 6)
    def _():
        for row in range(8):
            greet(row, brick_next)

    copies = {}

    def send(slot, src, dst, device):
        copy = pltpu.make_async_remote_copy(
            src_ref=src, dst_ref=dst, send_sem=send_sem.at[slot], recv_sem=recv_sem.at[slot],
            device_id=(device, g), device_id_type=pl.DeviceIdType.MESH,
        )
        copy.start()
        copies[slot] = copy

    def half(ref, which):
        return ref.at[core, pl.ds(0, KB), pl.ds(which * BLK, BLK)]

    def far_part(ref, which):
        return ref.at[core, pl.ds(0, KB), pl.ds(which * HALF, HALF)]

    def near_part(ref, block, which):
        return ref.at[core, pl.ds(0, KB), pl.ds(block * BLK + which * HALF, HALF)]

    def x_rows(origin):
        return x_all.at[pl.ds(2 * origin, 2), pl.ds(0, NZ)]

    def x_row(origin, i):
        return x_all.at[2 * origin + i, pl.ds(0, NZ)]

    def t_rows(origin):
        return table.at[pl.ds(2 * origin, 2)]

    pltpu.make_async_copy(h_own.at[core], h_own.at[core], own_sem).wait()
    pl.semaphore_wait(barrier, 15)
    for slot, ref, device in ((H_DN, h_dn, up), (H_UP, h_up, dn), (H_SIB, h_own, sib)):
        send(slot, half(h_own, 0), half(ref, 0), device)

    lane = lax.broadcasted_iota(jnp.int32, (8, BLK), 1)
    for i in range(2):
        first = jnp.full((8, BLK), NZ, jnp.int32)
        for z in reversed(range(NZ)):
            first = jnp.where(lane == cols_in[i, z], z, first)
        table[2 * r + i] = first
        for z in range(NZ):
            block = x_in[i, z].astype(jnp.float32)
            for v in range(z + 1, NZ):
                same = (cols_in[i, v] == cols_in[i, z]).astype(jnp.int32).astype(jnp.float32)
                block += x_in[i, v].astype(jnp.float32) * same
            x_all[2 * r + i, z] = block.astype(jnp.bfloat16)
    for slot, device in ((X_DN, up), (X_UP, dn), (X_SIB, sib)):
        send(slot, x_rows(r), x_rows(r), device)
    for slot, device in ((T_DN, up), (T_UP, dn), (T_SIB, sib)):
        send(slot, t_rows(r), t_rows(r), device)
    for slot, ref, device in ((H_DN, h_dn, up), (H_UP, h_up, dn), (H_SIB, h_own, sib)):
        send(slot + 1, half(h_own, 1), half(ref, 1), device)
    phi_copy = pltpu.make_async_copy(phi_in, phi, phi_sem)
    phi_copy.start()
    for i in range(KB):
        x_all[i, NZ] = jnp.zeros((BLK, BLK), jnp.bfloat16)

    def item_for(source, owner):
        found = sum(k * (owners[source, k] == owner).astype(jnp.int32) for k in range(1, SUB_DEV))
        return jnp.minimum(found, SUB_DEV - 1)

    count = jnp.int32(0)
    slot_source = [jnp.int32(0)] * OWN_MAX
    for source in range(16):
        has = sum((owners[source, k] == g).astype(jnp.int32) for k in range(SUB_DEV))
        has = jnp.minimum(has, 1)
        for t in range(OWN_MAX):
            slot_source[t] += source * has * (count == t).astype(jnp.int32)
        count += has

    def relay_h(block):
        far, far_ref = (H_FAR_A, h_far_a) if block == 0 else (H_FAR_B, h_far_b)
        copies[H_DN + block].wait_recv()
        send(far, near_part(h_dn, block, 0), far_part(far_ref, 0), up)
        send(H_SDN + block, half(h_dn, block), half(h_dn, block), sib)
        copies[H_UP + block].wait_recv()
        send(far + 1, near_part(h_up, block, 1), far_part(far_ref, 1), dn)
        send(H_SUP + block, half(h_up, block), half(h_up, block), sib)

    far = 2 * y_far + core
    copies[X_DN].wait_recv()
    send(X_FAR_A, x_row(dn, 0), x_row(dn, 0), up)
    send(X_SDN, x_rows(dn), x_rows(dn), sib)
    copies[X_UP].wait_recv()
    send(X_FAR_B, x_row(up, 1), x_row(up, 1), dn)
    send(X_SUP, x_rows(up), x_rows(up), sib)
    copies[T_DN].wait_recv()
    send(T_FAR, t_rows(dn), t_rows(dn), up)
    send(T_SDN, t_rows(dn), t_rows(dn), sib)
    copies[T_UP].wait_recv()
    send(T_SUP, t_rows(up), t_rows(up), sib)
    relay_h(0)
    copies[X_FAR_A].wait_recv()
    send(X_SFAR_A, x_row(far, 0), x_row(far, 0), sib)
    copies[X_FAR_B].wait_recv()
    send(X_SFAR_B, x_row(far, 1), x_row(far, 1), sib)
    copies[T_FAR].wait_recv()
    send(T_SFAR, t_rows(far), t_rows(far), sib)

    for slot in (X_SIB, X_SDN, X_SUP, X_SFAR_A, X_SFAR_B, T_SIB, T_SDN, T_SUP, T_SFAR):
        copies[slot].wait_recv()
    table_copy = pltpu.make_async_copy(table, table_s, table_sem)
    table_copy.start()
    table_copy.wait()

    def pick_blocks(k, h_ref, chip, blocks):
        for b in range(SUB_BLK):
            pick = picks[k, b]
            rows = slice(b * BLK, (b + 1) * BLK)
            for c in range(2):
                for n, block in enumerate(blocks):
                    z = table_s[pick, 0, 4 * chip + 2 * c + block]
                    at = (c * len(blocks) + n) * BLK
                    lhs[rows, at : at + BLK] = x_all[pick, z]
                depth = len(blocks) * BLK
                rhs[c * depth : (c + 1) * depth, rows] = h_ref[c, pick]

    def accumulate(h_ref, chip, blocks, first):
        depth = 2 * len(blocks) * BLK

        def one(k, carry):
            pick_blocks(k, h_ref, chip, blocks)
            part = jnp.dot(lhs[:, :depth], rhs[:depth, :], preferred_element_type=jnp.float32)
            if first:
                total[k] = part
            else:
                total[k] += part
            return carry

        lax.fori_loop(0, SUB_DEV, one, 0)

    copies[H_SIB].wait_recv()
    copies[H_SIB + 1].wait_recv()
    accumulate(h_own, y, (0, 1), True)
    relay_h(1)
    for ref, slot, chip in ((h_dn, H_SDN, y_dn), (h_up, H_SUP, y_up)):
        copies[slot].wait_recv()
        copies[slot + 1].wait_recv()
        accumulate(ref, chip, (0, 1), False)
    for far, passed, ref in ((H_FAR_A, H_SFAR_A, h_far_a), (H_FAR_B, H_SFAR_B, h_far_b)):
        for which in range(2):
            copies[far + which].wait_recv()
            send(passed + which, far_part(ref, which), far_part(ref, which), sib)
        for which in range(2):
            copies[passed + which].wait_recv()
        if far == H_FAR_A:
            accumulate(ref, y_far, (0,), False)

    mu = mu_in[0]

    class Way:
        def __init__(self, line, me, prev, nxt, swap_me, swap_prev, swap_nxt, x_first, bufs, base):
            self.own, self.nxt, self.prev, self.far = line
            self.me, self.to_prev, self.to_nxt = me, prev, nxt
            self.swap_me, self.swap_prev, self.swap_nxt = swap_me, swap_prev, swap_nxt
            self.x_first = x_first
            self.pack, self.passed, self.got = bufs
            self.base = base

        def grid(self, line_place, swap_place):
            if self.x_first:
                return 4 * swap_place + line_place
            return 4 * line_place + swap_place

        def line_copy(self, kind, k):
            rows = (pl.ds(0, SPLIT), pl.ds(0, SPLIT), pl.ds(0, SPLIT // 2), pl.ds(SPLIT // 2, SPLIT // 2))
            src = (self.own, self.own, self.prev, self.nxt)[kind]
            dst = (self.prev, self.nxt, self.far, self.far)[kind]
            slot = 4 * self.base + kind
            return pltpu.make_async_remote_copy(
                src_ref=src.at[k, rows[kind]], dst_ref=dst.at[k, rows[kind]],
                send_sem=line_send.at[slot, k], recv_sem=line_recv.at[slot, k],
                device_id=(r, (self.to_nxt, self.to_prev, self.to_nxt, self.to_prev)[kind]),
                device_id_type=pl.DeviceIdType.MESH,
            )

        def fill(self, slot):
            buf, place = (
                (self.own, 0), (self.nxt, 1), (self.prev, 3), (self.far, 2)
            )[slot]
            source = self.grid(lax.rem(self.me + place, 4), self.swap_me)
            for step in (2, 1, 3):
                owner = self.grid(self.me, lax.rem(self.swap_me + step, 4))
                self.pack[step - 1, slot] = buf[item_for(source, owner)]
            self.got[0, slot] = buf[item_for(source, g)]

        def swap(self, group, kind):
            slots = (pl.ds(0, 1), pl.ds(1, 2), pl.ds(3, 1))[group]
            top, low = pl.ds(0, SPLIT // 2), pl.ds(SPLIT // 2, SPLIT // 2)
            src, dst, device = (
                (self.pack.at[1, slots, top], self.passed.at[0, slots], self.swap_nxt),
                (self.pack.at[1, slots, low], self.passed.at[1, slots], self.swap_prev),
                (self.pack.at[0, slots], self.got.at[3, slots], self.swap_nxt),
                (self.pack.at[2, slots], self.got.at[1, slots], self.swap_prev),
                (self.passed.at[0, slots], self.got.at[2, slots, top], self.swap_nxt),
                (self.passed.at[1, slots], self.got.at[2, slots, low], self.swap_prev),
            )[kind]
            slot = 6 * (3 * self.base + group) + kind
            return pltpu.make_async_remote_copy(
                src_ref=src, dst_ref=dst,
                send_sem=swap_send.at[slot], recv_sem=swap_recv.at[slot],
                device_id=(r, device), device_id_type=pl.DeviceIdType.MESH,
            )

    along_x = Way(line_x, gx, x_prev, x_next, gz, z_prev, z_next, True, (pack_x, pass_x, got_x), 0)
    along_z = Way(line_z, gz, z_prev, z_next, gx, x_prev, x_next, False, (pack_z, pass_z, got_z), 1)
    ways = (along_x, along_z)

    def pass_on(k):
        for way in ways:
            way.line_copy(0, k).wait_recv()
            way.line_copy(2, k).start()
            way.line_copy(1, k).wait_recv()
            way.line_copy(3, k).start()

    def swap_out(group, slots):
        for way in ways:
            for slot in slots:
                way.fill(slot)
        for kind in range(4):
            for way in ways:
                way.swap(group, kind).start()

    def swap_on(group):
        for kind in range(2):
            for way in ways:
                way.swap(group, kind).wait_recv()
                way.swap(group, kind + 4).start()

    def sign(k, carry):
        pick_blocks(k, h_far_b, y_far, (1,))
        norm = jnp.zeros((1, TILE), jnp.float32)
        for n in range(3):
            cols = slice(n * TILE, (n + 1) * TILE)
            part = jnp.dot(
                lhs[:, :TILE], rhs[:TILE, cols], preferred_element_type=jnp.float32
            )
            mat = (total[k, :, cols] + part).astype(jnp.bfloat16).astype(jnp.float32)
            shifted = mat - jnp.where(eye_like(ORDER, TILE, -n * TILE), mu, 0.0)
            norm += jnp.sum(shifted * shifted, axis=0, keepdims=True)
            w[:, cols] = shifted.astype(jnp.bfloat16)
        square_scale = jnp.sum(norm, axis=1, keepdims=True) / ORDER + 1e-06
        scale_y = 0.25 / square_scale
        scale_z = 0.25 / jnp.sqrt(square_scale)
        for n in range(3):
            cols = slice(n * TILE, (n + 1) * TILE)
            square = jnp.dot(w[...], w[:, cols], preferred_element_type=jnp.float32)
            diag = jnp.where(eye_like(ORDER, TILE, -n * TILE), 3.0, 0.0)
            y0[:, cols] = (diag - scale_y * square).astype(jnp.bfloat16)
        for n in range(3):
            cols = slice(n * TILE, (n + 1) * TILE)
            step = jnp.dot(w[...], y0[:, cols], preferred_element_type=jnp.float32)
            z1[:, cols] = (scale_z * step).astype(jnp.bfloat16)
        square = jnp.dot(z1[...], z1[:, :BLK], preferred_element_type=jnp.float32)
        eye = eye_like(ORDER, BLK, 0)
        y1[...] = (jnp.where(eye, 3.0, 0.0) - square).astype(jnp.bfloat16)
        last = 0.5 * jnp.dot(z1[...], y1[...], preferred_element_type=jnp.float32)
        columns = (0.5 * (jnp.where(eye, 1.0, 0.0) - last)).astype(jnp.bfloat16)
        along_x.own[k] = columns[:SPLIT]
        along_z.own[k] = columns[SPLIT:]
        for way in ways:
            way.line_copy(0, k).start()
            way.line_copy(1, k).start()

        @pl.when(k > 0)
        def _():
            pass_on(k - 1)

        return carry

    lax.fori_loop(0, SUB_DEV, sign, 0)
    swap_out(0, (0,))
    pass_on(SUB_DEV - 1)
    swap_out(1, (1, 2))
    swap_on(0)
    for k in range(SUB_DEV):
        for way in ways:
            way.line_copy(2, k).wait_recv()
            way.line_copy(3, k).wait_recv()
    swap_out(2, (3,))
    swap_on(1)
    swap_on(2)
    for group in range(3):
        for kind in range(2, 6):
            for way in ways:
                way.swap(group, kind).wait_recv()
    phi_copy.wait()

    def slot_of(place):
        return place + (place == 2).astype(jnp.int32) - (place == 3).astype(jnp.int32)

    across = (((0,), (0,)), ((), ()))
    window = jnp.zeros((1, EXT), jnp.float32)
    for t in range(OWN_MAX):
        from_z = slot_source[t] // 4
        from_x = lax.rem(slot_source[t] - 4 * from_z + 4 - gx, 4)
        from_z = lax.rem(from_z + 4 - gz, 4)
        column[:SPLIT] = got_x[from_z, slot_of(from_x)]
        column[SPLIT:] = got_z[from_x, slot_of(from_z)]
        proj = lax.dot_general(column[...], phi[t], across, preferred_element_type=jnp.float32)
        values = jnp.sum(proj * phi[t, :BLK].astype(jnp.float32), axis=0, keepdims=True)
        window += values * (count > t).astype(jnp.int32).astype(jnp.float32)
    for i in range(EXT // BLK):
        pieces[i] = window[:, i * BLK : (i + 1) * BLK]

    def give(slot, piece, place, row, grid):
        copy = pltpu.make_async_remote_copy(
            src_ref=pieces.at[piece], dst_ref=sums.at[place],
            send_sem=sum_send.at[slot], recv_sem=sum_recv.at[place],
            device_id=(row, grid), device_id_type=pl.DeviceIdType.MESH,
        )
        copy.start()
        return copy

    given = []
    for row in range(2):
        given.append(give(7 + row, 10 + row, 8 + r, row, brick_next))
        given.append(give(9 + row, row, 8 + r, 6 + row, brick_prev))
    for step in range(1, 8):
        row = lax.rem(r + step, 8)
        given.append(give(step - 1, 2 + row, r, row, g))
    sums[r] = pieces[2 + r]

    def arrived(place):
        pltpu.make_async_copy(sums.at[place], sums.at[place], sum_recv.at[place]).wait()

    for step in range(1, 8):
        arrived(lax.rem(r + step, 8))

    @pl.when((r < 2) | (r >= 6))
    def _():
        for row in range(8):
            arrived(8 + row)

    out[...] = jnp.sum(sums[...], axis=0)
    for copy in (*copies.values(), *given):
        copy.wait_send()
    for way in ways:
        for kind in range(4):
            for k in range(SUB_DEV):
                way.line_copy(kind, k).wait_send()
        for kind in range(6):
            for group in range(3):
                way.swap(group, kind).wait_send()


def region(h_rows, x_blocks, x_cols, picks, owners, mu, orbitals):
    vmem = pl.BlockSpec(memory_space=pltpu.VMEM)
    smem = pl.BlockSpec(memory_space=pltpu.SMEM)
    hbm = pl.BlockSpec(memory_space=pl.ANY)
    h_buf = pltpu.VMEM((2, KB, 2 * BLK, BLK), jnp.bfloat16)
    h_far = pltpu.VMEM((2, KB, BLK, BLK), jnp.bfloat16)
    square = pltpu.VMEM((ORDER, ORDER), jnp.bfloat16)
    columns = pltpu.VMEM((ORDER, BLK), jnp.bfloat16)
    line = [pltpu.VMEM((SUB_DEV, SPLIT, BLK), jnp.bfloat16)] * 4
    pack = pltpu.VMEM((3, 4, SPLIT, BLK), jnp.bfloat16)
    slots4 = pltpu.VMEM((4, 4, SPLIT, BLK), jnp.bfloat16)
    passed = pltpu.VMEM((2, 4, SPLIT // 2, BLK), jnp.bfloat16)
    dma = pltpu.SemaphoreType.DMA
    return pl.pallas_call(
        region_kernel,
        out_shape=jax.ShapeDtypeStruct((1, BLK), jnp.float32),
        in_specs=[hbm, vmem, smem, smem, smem, smem, hbm],
        out_specs=vmem,
        scratch_shapes=[
            h_buf, h_buf, h_buf, h_far, h_far,
            pltpu.VMEM((KB, NZ + 1, BLK, BLK), jnp.bfloat16),
            pltpu.VMEM((KB, 8, BLK), jnp.int32),
            pltpu.SMEM((KB, 8, BLK), jnp.int32),
            pltpu.VMEM((ORDER, 4 * BLK), jnp.bfloat16),
            pltpu.VMEM((4 * BLK, ORDER), jnp.bfloat16),
            pltpu.VMEM((SUB_DEV, ORDER, ORDER), jnp.float32),
            square, square, square, columns,
            pltpu.VMEM((OWN_MAX, ORDER, EXT), jnp.bfloat16),
            line, line, pack, pack, passed, passed, slots4, slots4, columns,
            pltpu.VMEM((EXT // BLK, 1, BLK), jnp.float32),
            pltpu.VMEM((16, 1, BLK), jnp.float32),
            dma((N_SEM,)), dma((N_SEM,)), dma, dma, dma,
            dma((8, SUB_DEV)), dma((8, SUB_DEV)), dma((36,)), dma((36,)), dma((11,)), dma((16,)),
        ],
        compiler_params=pltpu.CompilerParams(
            collective_id=0, has_side_effects=True, vmem_limit_bytes=60 << 20
        ),
        name="region",
    )(h_rows, x_blocks, x_cols, picks, owners, mu, orbitals)


def on_device(h_rows, x_blocks, x_cols, sub_blocks, owners, shift_mu, orbitals):
    return region(
        h_rows[0], x_blocks[0], x_cols[0], sub_blocks[0, 0], owners[0], shift_mu, orbitals[0, 0]
    )


def solution(mesh):
    in_specs = (
        P("grid", "row", None),
        P("grid", "row", None, None, None),
        P("grid", "row", None),
        P("row", "grid", None, None),
        P("row", None, None),
        P(),
        P("row", "grid", None, None, None),
    )
    out_specs = P("grid", "row")
    return jax.shard_map(
        on_device, mesh=mesh, in_specs=in_specs, out_specs=out_specs, check_vma=False
    )
```

```python
import jax
import jax.numpy as jnp
from jax import lax
from jax.experimental import pallas as pl
from jax.experimental.pallas import tpu as pltpu
from jax.sharding import PartitionSpec as P

BLK = 128
SUB_BLK = 6
NZ = 8
SUB_DEV = 3
OWN_MAX = 6
PLANE = 256
DEPTH = 4
MARG = 1
ORDER = 768
KB = 16
NREG = 2048
HALF = 64
TILE = 256
SPLIT = 384
EXT = 1536

X_DN, X_UP, X_SIB, X_FAR_A, X_FAR_B, X_SDN, X_SUP, X_SFAR_A, X_SFAR_B = range(9)
T_DN, T_UP, T_SIB, T_FAR, T_SDN, T_SUP, T_SFAR = range(9, 16)
H_DN, H_UP, H_SIB, H_SDN, H_SUP, H_FAR_A, H_FAR_B, H_SFAR_A, H_SFAR_B = range(16, 34, 2)
N_SEM = 34


def eye_like(rows, cols, first_row):
    row = lax.broadcasted_iota(jnp.int32, (rows, cols), 0) + first_row
    col = lax.broadcasted_iota(jnp.int32, (rows, cols), 1)
    return row == col


def region_kernel(
    h_in, x_in, cols_in, picks, owners, mu_in, phi_in, out,
    h_own, h_dn, h_up, h_far_a, h_far_b, x_all, table, table_s, lhs, rhs, total, w, y0, z1, y1,
    phi, line_x, line_z, pack_x, pack_z, pass_x, pass_z, got_x, got_z, column, pieces, sums,
    send_sem, recv_sem, own_sem, table_sem, phi_sem,
    line_send, line_recv, swap_send, swap_recv, sum_send, sum_recv,
):
    r = lax.axis_index("row")
    g = lax.axis_index("grid")
    gz = g // 4
    gx = g - 4 * gz
    y = r // 2
    core = r - 2 * y
    sib = 2 * y + 1 - core
    y_up, y_dn, y_far = lax.rem(y + 1, 4), lax.rem(y + 3, 4), lax.rem(y + 2, 4)
    up, dn = 2 * y_up + core, 2 * y_dn + core
    x_next = 4 * gz + lax.rem(gx + 1, 4)
    x_prev = 4 * gz + lax.rem(gx + 3, 4)
    z_next = 4 * lax.rem(gz + 1, 4) + gx
    z_prev = 4 * lax.rem(gz + 3, 4) + gx
    brick_next = lax.rem(g + 1, 16)
    brick_prev = lax.rem(g + 15, 16)

    for b in range(KB):
        pltpu.make_async_copy(
            h_in.at[:, b * BLK : (b + 1) * BLK], h_own.at[core, b], own_sem
        ).start()
    sums[...] = jnp.zeros_like(sums)
    barrier = pltpu.get_barrier_semaphore()

    def greet(row, grid):
        pl.semaphore_signal(
            barrier, inc=1, device_id=(row, grid), device_id_type=pl.DeviceIdType.MESH
        )

    for step in range(1, 8):
        greet(lax.rem(r + step, 8), g)
    for other in (x_next, x_prev, z_next, z_prev):
        greet(r, other)

    @pl.when(r < 2)
    def _():
        for row in range(8):
            greet(row, brick_prev)

    @pl.when(r >= 6)
    def _():
        for row in range(8):
            greet(row, brick_next)

    copies = {}

    def send(slot, src, dst, device):
        copy = pltpu.make_async_remote_copy(
            src_ref=src, dst_ref=dst, send_sem=send_sem.at[slot], recv_sem=recv_sem.at[slot],
            device_id=(device, g), device_id_type=pl.DeviceIdType.MESH,
        )
        copy.start()
        copies[slot] = copy

    def half(ref, which):
        return ref.at[core, pl.ds(0, KB), pl.ds(which * BLK, BLK)]

    def far_part(ref, which):
        return ref.at[core, pl.ds(0, KB), pl.ds(which * HALF, HALF)]

    def near_part(ref, block, which):
        return ref.at[core, pl.ds(0, KB), pl.ds(block * BLK + which * HALF, HALF)]

    def x_rows(origin):
        return x_all.at[pl.ds(2 * origin, 2), pl.ds(0, NZ)]

    def x_row(origin, i):
        return x_all.at[2 * origin + i, pl.ds(0, NZ)]

    def t_rows(origin):
        return table.at[pl.ds(2 * origin, 2)]

    pltpu.make_async_copy(h_own.at[core], h_own.at[core], own_sem).wait()
    pl.semaphore_wait(barrier, 15)
    for slot, ref, device in ((H_DN, h_dn, up), (H_UP, h_up, dn), (H_SIB, h_own, sib)):
        send(slot, half(h_own, 0), half(ref, 0), device)

    lane = lax.broadcasted_iota(jnp.int32, (8, BLK), 1)
    for i in range(2):
        first = jnp.full((8, BLK), NZ, jnp.int32)
        for z in reversed(range(NZ)):
            first = jnp.where(lane == cols_in[i, z], z, first)
        table[2 * r + i] = first
        for z in range(NZ):
            block = x_in[i, z].astype(jnp.float32)
            for v in range(z + 1, NZ):
                same = (cols_in[i, v] == cols_in[i, z]).astype(jnp.int32).astype(jnp.float32)
                block += x_in[i, v].astype(jnp.float32) * same
            x_all[2 * r + i, z] = block.astype(jnp.bfloat16)
    for slot, device in ((X_DN, up), (X_UP, dn), (X_SIB, sib)):
        send(slot, x_rows(r), x_rows(r), device)
    for slot, device in ((T_DN, up), (T_UP, dn), (T_SIB, sib)):
        send(slot, t_rows(r), t_rows(r), device)
    for slot, ref, device in ((H_DN, h_dn, up), (H_UP, h_up, dn), (H_SIB, h_own, sib)):
        send(slot + 1, half(h_own, 1), half(ref, 1), device)
    phi_copy = pltpu.make_async_copy(phi_in, phi, phi_sem)
    phi_copy.start()
    for i in range(KB):
        x_all[i, NZ] = jnp.zeros((BLK, BLK), jnp.bfloat16)

    def item_for(source, owner):
        found = sum(k * (owners[k, 0, source] == owner).astype(jnp.int32) for k in range(1, SUB_DEV))
        return jnp.minimum(found, SUB_DEV - 1)

    count = jnp.int32(0)
    slot_source = [jnp.int32(0)] * OWN_MAX
    for source in range(16):
        has = sum((owners[k, 0, source] == g).astype(jnp.int32) for k in range(SUB_DEV))
        has = jnp.minimum(has, 1)
        for t in range(OWN_MAX):
            slot_source[t] += source * has * (count == t).astype(jnp.int32)
        count += has

    def relay_h(block):
        far, far_ref = (H_FAR_A, h_far_a) if block == 0 else (H_FAR_B, h_far_b)
        copies[H_DN + block].wait_recv()
        send(far, near_part(h_dn, block, 0), far_part(far_ref, 0), up)
        send(H_SDN + block, half(h_dn, block), half(h_dn, block), sib)
        copies[H_UP + block].wait_recv()
        send(far + 1, near_part(h_up, block, 1), far_part(far_ref, 1), dn)
        send(H_SUP + block, half(h_up, block), half(h_up, block), sib)

    far = 2 * y_far + core
    copies[X_DN].wait_recv()
    send(X_FAR_A, x_row(dn, 0), x_row(dn, 0), up)
    send(X_SDN, x_rows(dn), x_rows(dn), sib)
    copies[X_UP].wait_recv()
    send(X_FAR_B, x_row(up, 1), x_row(up, 1), dn)
    send(X_SUP, x_rows(up), x_rows(up), sib)
    copies[T_DN].wait_recv()
    send(T_FAR, t_rows(dn), t_rows(dn), up)
    send(T_SDN, t_rows(dn), t_rows(dn), sib)
    copies[T_UP].wait_recv()
    send(T_SUP, t_rows(up), t_rows(up), sib)
    relay_h(0)
    copies[X_FAR_A].wait_recv()
    send(X_SFAR_A, x_row(far, 0), x_row(far, 0), sib)
    copies[X_FAR_B].wait_recv()
    send(X_SFAR_B, x_row(far, 1), x_row(far, 1), sib)
    copies[T_FAR].wait_recv()
    send(T_SFAR, t_rows(far), t_rows(far), sib)

    for slot in (X_SIB, X_SDN, X_SUP, X_SFAR_A, X_SFAR_B, T_SIB, T_SDN, T_SUP, T_SFAR):
        copies[slot].wait_recv()
    table_copy = pltpu.make_async_copy(table, table_s, table_sem)
    table_copy.start()
    table_copy.wait()

    def pick_blocks(k, h_ref, chip, blocks):
        for b in range(SUB_BLK):
            pick = picks[k, 0, b]
            rows = slice(b * BLK, (b + 1) * BLK)
            for c in range(2):
                for n, block in enumerate(blocks):
                    z = table_s[pick, 0, 4 * chip + 2 * c + block]
                    at = (c * len(blocks) + n) * BLK
                    lhs[rows, at : at + BLK] = x_all[pick, z]
                depth = len(blocks) * BLK
                rhs[c * depth : (c + 1) * depth, rows] = h_ref[c, pick]

    def accumulate(h_ref, chip, blocks, first):
        depth = 2 * len(blocks) * BLK

        def one(k, carry):
            pick_blocks(k, h_ref, chip, blocks)
            part = jnp.dot(lhs[:, :depth], rhs[:depth, :], preferred_element_type=jnp.float32)
            if first:
                total[k] = part
            else:
                total[k] += part
            return carry

        lax.fori_loop(0, SUB_DEV, one, 0)

    copies[H_SIB].wait_recv()
    copies[H_SIB + 1].wait_recv()
    accumulate(h_own, y, (0, 1), True)
    relay_h(1)
    for ref, slot, chip in ((h_dn, H_SDN, y_dn), (h_up, H_SUP, y_up)):
        copies[slot].wait_recv()
        copies[slot + 1].wait_recv()
        accumulate(ref, chip, (0, 1), False)
    for far, passed, ref in ((H_FAR_A, H_SFAR_A, h_far_a), (H_FAR_B, H_SFAR_B, h_far_b)):
        for which in range(2):
            copies[far + which].wait_recv()
            send(passed + which, far_part(ref, which), far_part(ref, which), sib)
        for which in range(2):
            copies[passed + which].wait_recv()
        if far == H_FAR_A:
            accumulate(ref, y_far, (0,), False)

    mu = mu_in[0, 0]

    class Way:
        def __init__(self, line, me, prev, nxt, swap_me, swap_prev, swap_nxt, x_first, bufs, base):
            self.own, self.nxt, self.prev, self.far = line
            self.me, self.to_prev, self.to_nxt = me, prev, nxt
            self.swap_me, self.swap_prev, self.swap_nxt = swap_me, swap_prev, swap_nxt
            self.x_first = x_first
            self.pack, self.passed, self.got = bufs
            self.base = base

        def grid(self, line_place, swap_place):
            if self.x_first:
                return 4 * swap_place + line_place
            return 4 * line_place + swap_place

        def line_copy(self, kind, k):
            rows = (pl.ds(0, SPLIT), pl.ds(0, SPLIT), pl.ds(0, SPLIT // 2), pl.ds(SPLIT // 2, SPLIT // 2))
            src = (self.own, self.own, self.prev, self.nxt)[kind]
            dst = (self.prev, self.nxt, self.far, self.far)[kind]
            slot = 4 * self.base + kind
            return pltpu.make_async_remote_copy(
                src_ref=src.at[k, rows[kind]], dst_ref=dst.at[k, rows[kind]],
                send_sem=line_send.at[slot, k], recv_sem=line_recv.at[slot, k],
                device_id=(r, (self.to_nxt, self.to_prev, self.to_nxt, self.to_prev)[kind]),
                device_id_type=pl.DeviceIdType.MESH,
            )

        def fill(self, slot):
            buf, place = (
                (self.own, 0), (self.nxt, 1), (self.prev, 3), (self.far, 2)
            )[slot]
            source = self.grid(lax.rem(self.me + place, 4), self.swap_me)
            for step in (2, 1, 3):
                owner = self.grid(self.me, lax.rem(self.swap_me + step, 4))
                self.pack[step - 1, slot] = buf[item_for(source, owner)]
            self.got[0, slot] = buf[item_for(source, g)]

        def swap(self, group, kind):
            slots = (pl.ds(0, 1), pl.ds(1, 2), pl.ds(3, 1))[group]
            top, low = pl.ds(0, SPLIT // 2), pl.ds(SPLIT // 2, SPLIT // 2)
            src, dst, device = (
                (self.pack.at[1, slots, top], self.passed.at[0, slots], self.swap_nxt),
                (self.pack.at[1, slots, low], self.passed.at[1, slots], self.swap_prev),
                (self.pack.at[0, slots], self.got.at[3, slots], self.swap_nxt),
                (self.pack.at[2, slots], self.got.at[1, slots], self.swap_prev),
                (self.passed.at[0, slots], self.got.at[2, slots, top], self.swap_nxt),
                (self.passed.at[1, slots], self.got.at[2, slots, low], self.swap_prev),
            )[kind]
            slot = 6 * (3 * self.base + group) + kind
            return pltpu.make_async_remote_copy(
                src_ref=src, dst_ref=dst,
                send_sem=swap_send.at[slot], recv_sem=swap_recv.at[slot],
                device_id=(r, device), device_id_type=pl.DeviceIdType.MESH,
            )

    along_x = Way(line_x, gx, x_prev, x_next, gz, z_prev, z_next, True, (pack_x, pass_x, got_x), 0)
    along_z = Way(line_z, gz, z_prev, z_next, gx, x_prev, x_next, False, (pack_z, pass_z, got_z), 1)
    ways = (along_x, along_z)

    def pass_on(k):
        for way in ways:
            way.line_copy(0, k).wait_recv()
            way.line_copy(2, k).start()
            way.line_copy(1, k).wait_recv()
            way.line_copy(3, k).start()

    def swap_out(group, slots):
        for way in ways:
            for slot in slots:
                way.fill(slot)
        for kind in range(4):
            for way in ways:
                way.swap(group, kind).start()

    def swap_on(group):
        for kind in range(2):
            for way in ways:
                way.swap(group, kind).wait_recv()
                way.swap(group, kind + 4).start()

    def sign(k, carry):
        pick_blocks(k, h_far_b, y_far, (1,))
        norm = jnp.zeros((1, TILE), jnp.float32)
        for n in range(3):
            cols = slice(n * TILE, (n + 1) * TILE)
            part = jnp.dot(
                lhs[:, :TILE], rhs[:TILE, cols], preferred_element_type=jnp.float32
            )
            mat = (total[k, :, cols] + part).astype(jnp.bfloat16).astype(jnp.float32)
            shifted = mat - jnp.where(eye_like(ORDER, TILE, -n * TILE), mu, 0.0)
            norm += jnp.sum(shifted * shifted, axis=0, keepdims=True)
            w[:, cols] = shifted.astype(jnp.bfloat16)
        square_scale = jnp.sum(norm, axis=1, keepdims=True) / ORDER + 1e-06
        scale_y = 0.25 / square_scale
        scale_z = 0.25 / jnp.sqrt(square_scale)
        for n in range(3):
            cols = slice(n * TILE, (n + 1) * TILE)
            square = jnp.dot(w[...], w[:, cols], preferred_element_type=jnp.float32)
            diag = jnp.where(eye_like(ORDER, TILE, -n * TILE), 3.0, 0.0)
            y0[:, cols] = (diag - scale_y * square).astype(jnp.bfloat16)
        for n in range(3):
            cols = slice(n * TILE, (n + 1) * TILE)
            step = jnp.dot(w[...], y0[:, cols], preferred_element_type=jnp.float32)
            z1[:, cols] = (scale_z * step).astype(jnp.bfloat16)
        square = jnp.dot(z1[...], z1[:, :BLK], preferred_element_type=jnp.float32)
        eye = eye_like(ORDER, BLK, 0)
        y1[...] = (jnp.where(eye, 3.0, 0.0) - square).astype(jnp.bfloat16)
        last = 0.5 * jnp.dot(z1[...], y1[...], preferred_element_type=jnp.float32)
        columns = (0.5 * (jnp.where(eye, 1.0, 0.0) - last)).astype(jnp.bfloat16)
        along_x.own[k] = columns[:SPLIT]
        along_z.own[k] = columns[SPLIT:]
        for way in ways:
            way.line_copy(0, k).start()
            way.line_copy(1, k).start()

        @pl.when(k > 0)
        def _():
            pass_on(k - 1)

        return carry

    lax.fori_loop(0, SUB_DEV, sign, 0)
    swap_out(0, (0,))
    pass_on(SUB_DEV - 1)
    swap_out(1, (1, 2))
    swap_on(0)
    for k in range(SUB_DEV):
        for way in ways:
            way.line_copy(2, k).wait_recv()
            way.line_copy(3, k).wait_recv()
    swap_out(2, (3,))
    swap_on(1)
    swap_on(2)
    for group in range(3):
        for kind in range(2, 6):
            for way in ways:
                way.swap(group, kind).wait_recv()
    phi_copy.wait()

    def slot_of(place):
        return place + (place == 2).astype(jnp.int32) - (place == 3).astype(jnp.int32)

    across = (((0,), (0,)), ((), ()))
    window = jnp.zeros((1, EXT), jnp.float32)
    for t in range(OWN_MAX):
        from_z = slot_source[t] // 4
        from_x = lax.rem(slot_source[t] - 4 * from_z + 4 - gx, 4)
        from_z = lax.rem(from_z + 4 - gz, 4)
        column[:SPLIT] = got_x[from_z, slot_of(from_x)]
        column[SPLIT:] = got_z[from_x, slot_of(from_z)]
        proj = lax.dot_general(column[...], phi[t], across, preferred_element_type=jnp.float32)
        values = jnp.sum(proj * phi[t, :BLK].astype(jnp.float32), axis=0, keepdims=True)
        window += values * (count > t).astype(jnp.int32).astype(jnp.float32)
    for i in range(EXT // BLK):
        pieces[i] = window[:, i * BLK : (i + 1) * BLK]

    def give(slot, piece, place, row, grid):
        copy = pltpu.make_async_remote_copy(
            src_ref=pieces.at[piece], dst_ref=sums.at[place],
            send_sem=sum_send.at[slot], recv_sem=sum_recv.at[place],
            device_id=(row, grid), device_id_type=pl.DeviceIdType.MESH,
        )
        copy.start()
        return copy

    given = []
    for row in range(2):
        given.append(give(7 + row, 10 + row, 8 + r, row, brick_next))
        given.append(give(9 + row, row, 8 + r, 6 + row, brick_prev))
    for step in range(1, 8):
        row = lax.rem(r + step, 8)
        given.append(give(step - 1, 2 + row, r, row, g))
    sums[r] = pieces[2 + r]

    def arrived(place):
        pltpu.make_async_copy(sums.at[place], sums.at[place], sum_recv.at[place]).wait()

    for step in range(1, 8):
        arrived(lax.rem(r + step, 8))

    @pl.when((r < 2) | (r >= 6))
    def _():
        for row in range(8):
            arrived(8 + row)

    out[...] = jnp.sum(sums[...], axis=0)
    for copy in (*copies.values(), *given):
        copy.wait_send()
    for way in ways:
        for kind in range(4):
            for k in range(SUB_DEV):
                way.line_copy(kind, k).wait_send()
        for kind in range(6):
            for group in range(3):
                way.swap(group, kind).wait_send()


def region(h_rows, x_blocks, x_cols, picks, owners, mu, orbitals):
    vmem = pl.BlockSpec(memory_space=pltpu.VMEM)
    smem = pl.BlockSpec(memory_space=pltpu.SMEM)
    hbm = pl.BlockSpec(memory_space=pl.ANY)
    h_buf = pltpu.VMEM((2, KB, 2 * BLK, BLK), jnp.bfloat16)
    h_far = pltpu.VMEM((2, KB, BLK, BLK), jnp.bfloat16)
    square = pltpu.VMEM((ORDER, ORDER), jnp.bfloat16)
    columns = pltpu.VMEM((ORDER, BLK), jnp.bfloat16)
    line = [pltpu.VMEM((SUB_DEV, SPLIT, BLK), jnp.bfloat16)] * 4
    pack = pltpu.VMEM((3, 4, SPLIT, BLK), jnp.bfloat16)
    slots4 = pltpu.VMEM((4, 4, SPLIT, BLK), jnp.bfloat16)
    passed = pltpu.VMEM((2, 4, SPLIT // 2, BLK), jnp.bfloat16)
    dma = pltpu.SemaphoreType.DMA
    return pl.pallas_call(
        region_kernel,
        out_shape=jax.ShapeDtypeStruct((1, BLK), jnp.float32),
        in_specs=[hbm, vmem, smem, smem, smem, smem, hbm],
        out_specs=vmem,
        scratch_shapes=[
            h_buf, h_buf, h_buf, h_far, h_far,
            pltpu.VMEM((KB, NZ + 1, BLK, BLK), jnp.bfloat16),
            pltpu.VMEM((KB, 8, BLK), jnp.int32),
            pltpu.SMEM((KB, 8, BLK), jnp.int32),
            pltpu.VMEM((ORDER, 4 * BLK), jnp.bfloat16),
            pltpu.VMEM((4 * BLK, ORDER), jnp.bfloat16),
            pltpu.VMEM((SUB_DEV, ORDER, ORDER), jnp.float32),
            square, square, square, columns,
            pltpu.VMEM((OWN_MAX, ORDER, EXT), jnp.bfloat16),
            line, line, pack, pack, passed, passed, slots4, slots4, columns,
            pltpu.VMEM((EXT // BLK, 1, BLK), jnp.float32),
            pltpu.VMEM((16, 1, BLK), jnp.float32),
            dma((N_SEM,)), dma((N_SEM,)), dma, dma, dma,
            dma((8, SUB_DEV)), dma((8, SUB_DEV)), dma((36,)), dma((36,)), dma((11,)), dma((16,)),
        ],
        compiler_params=pltpu.CompilerParams(
            collective_id=0, has_side_effects=True, vmem_limit_bytes=60 << 20
        ),
        name="region",
    )(h_rows, x_blocks, x_cols, picks, owners, mu, orbitals)


def on_device(h_rows, x_blocks, x_cols, sub_blocks, owners, shift_mu, orbitals):
    return region(
        h_rows[0], x_blocks[0], x_cols[0], jnp.transpose(sub_blocks[0], (1, 0, 2)),
        jnp.transpose(owners, (2, 0, 1)), shift_mu.reshape(1, 1), orbitals[0, 0],
    )


def solution(mesh):
    in_specs = (
        P("grid", "row", None),
        P("grid", "row", None, None, None),
        P("grid", "row", None),
        P("row", "grid", None, None),
        P("row", None, None),
        P(),
        P("row", "grid", None, None, None),
    )
    out_specs = P("grid", "row")
    return jax.shard_map(
        on_device, mesh=mesh, in_specs=in_specs, out_specs=out_specs, check_vma=False
    )
```

```python
import jax
import jax.numpy as jnp
from jax import lax
from jax.experimental import pallas as pl
from jax.experimental.pallas import tpu as pltpu
from jax.sharding import PartitionSpec as P

BLK = 128
SUB_BLK = 6
NZ = 8
SUB_DEV = 3
OWN_MAX = 6
PLANE = 256
DEPTH = 4
MARG = 1
ORDER = 768
KB = 16
NREG = 2048
HALF = 64
TILE = 256
SPLIT = 384
EXT = 1536

X_DN, X_UP, X_SIB, X_FAR_A, X_FAR_B, X_SDN, X_SUP, X_SFAR_A, X_SFAR_B = range(9)
T_DN, T_UP, T_SIB, T_FAR, T_SDN, T_SUP, T_SFAR = range(9, 16)
H_DN, H_UP, H_SIB, H_SDN, H_SUP, H_FAR_A, H_FAR_B, H_SFAR_A, H_SFAR_B = range(16, 34, 2)
N_SEM = 34


def eye_like(rows, cols, first_row):
    row = lax.broadcasted_iota(jnp.int32, (rows, cols), 0) + first_row
    col = lax.broadcasted_iota(jnp.int32, (rows, cols), 1)
    return row == col


def region_kernel(
    h_in, x_in, cols_in, picks, owners, mu_in, phi_in, out,
    h_own, h_dn, h_up, h_far_a, h_far_b, x_all, table, table_s, lhs, rhs, total, w, y0, z1, y1,
    phi, line_x, line_z, pack_x, pack_z, pass_x, pass_z, got_x, got_z, column, pieces, sums,
    send_sem, recv_sem, own_sem, table_sem, phi_sem,
    line_send, line_recv, swap_send, swap_recv, sum_send, sum_recv,
):
    r = lax.axis_index("row")
    g = lax.axis_index("grid")
    gz = g // 4
    gx = g - 4 * gz
    y = r // 2
    core = r - 2 * y
    sib = 2 * y + 1 - core
    y_up, y_dn, y_far = lax.rem(y + 1, 4), lax.rem(y + 3, 4), lax.rem(y + 2, 4)
    up, dn = 2 * y_up + core, 2 * y_dn + core
    x_next = 4 * gz + lax.rem(gx + 1, 4)
    x_prev = 4 * gz + lax.rem(gx + 3, 4)
    z_next = 4 * lax.rem(gz + 1, 4) + gx
    z_prev = 4 * lax.rem(gz + 3, 4) + gx
    brick_next = lax.rem(g + 1, 16)
    brick_prev = lax.rem(g + 15, 16)

    for b in range(KB):
        pltpu.make_async_copy(
            h_in.at[:, b * BLK : (b + 1) * BLK], h_own.at[core, b], own_sem
        ).start()
    sums[...] = jnp.zeros_like(sums)
    barrier = pltpu.get_barrier_semaphore()

    def greet(row, grid):
        pl.semaphore_signal(
            barrier, inc=1, device_id=(row, grid), device_id_type=pl.DeviceIdType.MESH
        )

    for step in range(1, 8):
        greet(lax.rem(r + step, 8), g)
    for other in (x_next, x_prev, z_next, z_prev):
        greet(r, other)

    @pl.when(r < 2)
    def _():
        for row in range(8):
            greet(row, brick_prev)

    @pl.when(r >= 6)
    def _():
        for row in range(8):
            greet(row, brick_next)

    copies = {}

    def send(slot, src, dst, device):
        copy = pltpu.make_async_remote_copy(
            src_ref=src, dst_ref=dst, send_sem=send_sem.at[slot], recv_sem=recv_sem.at[slot],
            device_id=(device, g), device_id_type=pl.DeviceIdType.MESH,
        )
        copy.start()
        copies[slot] = copy

    def half(ref, which):
        return ref.at[core, pl.ds(0, KB), pl.ds(which * BLK, BLK)]

    def far_part(ref, which):
        return ref.at[core, pl.ds(0, KB), pl.ds(which * HALF, HALF)]

    def near_part(ref, block, which):
        return ref.at[core, pl.ds(0, KB), pl.ds(block * BLK + which * HALF, HALF)]

    def x_rows(origin):
        return x_all.at[pl.ds(2 * origin, 2), pl.ds(0, NZ)]

    def x_row(origin, i):
        return x_all.at[2 * origin + i, pl.ds(0, NZ)]

    def t_rows(origin):
        return table.at[pl.ds(2 * origin, 2)]

    pltpu.make_async_copy(h_own.at[core], h_own.at[core], own_sem).wait()
    pl.semaphore_wait(barrier, 15)
    for slot, ref, device in ((H_DN, h_dn, up), (H_UP, h_up, dn), (H_SIB, h_own, sib)):
        send(slot, half(h_own, 0), half(ref, 0), device)

    lane = lax.broadcasted_iota(jnp.int32, (8, BLK), 1)
    for i in range(2):
        first = jnp.full((8, BLK), NZ, jnp.int32)
        for z in reversed(range(NZ)):
            first = jnp.where(lane == cols_in[i, z], z, first)
        table[2 * r + i] = first
        for z in range(NZ):
            block = x_in[i, z].astype(jnp.float32)
            for v in range(z + 1, NZ):
                same = (cols_in[i, v] == cols_in[i, z]).astype(jnp.int32).astype(jnp.float32)
                block += x_in[i, v].astype(jnp.float32) * same
            x_all[2 * r + i, z] = block.astype(jnp.bfloat16)
    for slot, device in ((X_DN, up), (X_UP, dn), (X_SIB, sib)):
        send(slot, x_rows(r), x_rows(r), device)
    for slot, device in ((T_DN, up), (T_UP, dn), (T_SIB, sib)):
        send(slot, t_rows(r), t_rows(r), device)
    for slot, ref, device in ((H_DN, h_dn, up), (H_UP, h_up, dn), (H_SIB, h_own, sib)):
        send(slot + 1, half(h_own, 1), half(ref, 1), device)
    phi_copy = pltpu.make_async_copy(phi_in, phi, phi_sem)
    phi_copy.start()
    for i in range(KB):
        x_all[i, NZ] = jnp.zeros((BLK, BLK), jnp.bfloat16)

    def item_for(source, owner):
        found = sum(k * (owners[k, 0, source] == owner).astype(jnp.int32) for k in range(1, SUB_DEV))
        return jnp.minimum(found, SUB_DEV - 1)

    count = jnp.int32(0)
    slot_source = [jnp.int32(0)] * OWN_MAX
    for source in range(16):
        has = sum((owners[k, 0, source] == g).astype(jnp.int32) for k in range(SUB_DEV))
        has = jnp.minimum(has, 1)
        for t in range(OWN_MAX):
            slot_source[t] += source * has * (count == t).astype(jnp.int32)
        count += has

    def relay_h(block):
        far, far_ref = (H_FAR_A, h_far_a) if block == 0 else (H_FAR_B, h_far_b)
        copies[H_DN + block].wait_recv()
        send(far, near_part(h_dn, block, 0), far_part(far_ref, 0), up)
        send(H_SDN + block, half(h_dn, block), half(h_dn, block), sib)
        copies[H_UP + block].wait_recv()
        send(far + 1, near_part(h_up, block, 1), far_part(far_ref, 1), dn)
        send(H_SUP + block, half(h_up, block), half(h_up, block), sib)

    far = 2 * y_far + core
    copies[X_DN].wait_recv()
    send(X_FAR_A, x_row(dn, 0), x_row(dn, 0), up)
    send(X_SDN, x_rows(dn), x_rows(dn), sib)
    copies[X_UP].wait_recv()
    send(X_FAR_B, x_row(up, 1), x_row(up, 1), dn)
    send(X_SUP, x_rows(up), x_rows(up), sib)
    copies[T_DN].wait_recv()
    send(T_FAR, t_rows(dn), t_rows(dn), up)
    send(T_SDN, t_rows(dn), t_rows(dn), sib)
    copies[T_UP].wait_recv()
    send(T_SUP, t_rows(up), t_rows(up), sib)
    relay_h(0)
    copies[X_FAR_A].wait_recv()
    send(X_SFAR_A, x_row(far, 0), x_row(far, 0), sib)
    copies[X_FAR_B].wait_recv()
    send(X_SFAR_B, x_row(far, 1), x_row(far, 1), sib)
    copies[T_FAR].wait_recv()
    send(T_SFAR, t_rows(far), t_rows(far), sib)

    for slot in (X_SIB, X_SDN, X_SUP, X_SFAR_A, X_SFAR_B, T_SIB, T_SDN, T_SUP, T_SFAR):
        copies[slot].wait_recv()
    table_copy = pltpu.make_async_copy(table, table_s, table_sem)
    table_copy.start()
    table_copy.wait()

    def pick_blocks(k, h_ref, chip, blocks):
        for b in range(SUB_BLK):
            pick = picks[k, 0, b]
            rows = slice(b * BLK, (b + 1) * BLK)
            for c in range(2):
                for n, block in enumerate(blocks):
                    z = table_s[pick, 0, 4 * chip + 2 * c + block]
                    at = (c * len(blocks) + n) * BLK
                    lhs[rows, at : at + BLK] = x_all[pick, z]
                depth = len(blocks) * BLK
                rhs[c * depth : (c + 1) * depth, rows] = h_ref[c, pick]

    def accumulate(h_ref, chip, blocks, first):
        depth = 2 * len(blocks) * BLK

        def one(k, carry):
            pick_blocks(k, h_ref, chip, blocks)
            part = jnp.dot(lhs[:, :depth], rhs[:depth, :], preferred_element_type=jnp.float32)
            if first:
                total[k] = part
            else:
                total[k] += part
            return carry

        lax.fori_loop(0, SUB_DEV, one, 0)

    copies[H_SIB].wait_recv()
    copies[H_SIB + 1].wait_recv()
    accumulate(h_own, y, (0, 1), True)
    relay_h(1)
    for ref, slot, chip in ((h_dn, H_SDN, y_dn), (h_up, H_SUP, y_up)):
        copies[slot].wait_recv()
        copies[slot + 1].wait_recv()
        accumulate(ref, chip, (0, 1), False)
    for far, passed, ref in ((H_FAR_A, H_SFAR_A, h_far_a), (H_FAR_B, H_SFAR_B, h_far_b)):
        for which in range(2):
            copies[far + which].wait_recv()
            send(passed + which, far_part(ref, which), far_part(ref, which), sib)
        for which in range(2):
            copies[passed + which].wait_recv()
        if far == H_FAR_A:
            accumulate(ref, y_far, (0,), False)

    mu = mu_in[0, 0]

    class Way:
        def __init__(self, line, me, prev, nxt, swap_me, swap_prev, swap_nxt, x_first, bufs, base):
            self.own, self.nxt, self.prev, self.far = line
            self.me, self.to_prev, self.to_nxt = me, prev, nxt
            self.swap_me, self.swap_prev, self.swap_nxt = swap_me, swap_prev, swap_nxt
            self.x_first = x_first
            self.pack, self.passed, self.got = bufs
            self.base = base

        def grid(self, line_place, swap_place):
            if self.x_first:
                return 4 * swap_place + line_place
            return 4 * line_place + swap_place

        def line_copy(self, kind, k):
            rows = (pl.ds(0, SPLIT), pl.ds(0, SPLIT), pl.ds(0, SPLIT // 2), pl.ds(SPLIT // 2, SPLIT // 2))
            src = (self.own, self.own, self.prev, self.nxt)[kind]
            dst = (self.prev, self.nxt, self.far, self.far)[kind]
            slot = 4 * self.base + kind
            return pltpu.make_async_remote_copy(
                src_ref=src.at[k, rows[kind]], dst_ref=dst.at[k, rows[kind]],
                send_sem=line_send.at[slot, k], recv_sem=line_recv.at[slot, k],
                device_id=(r, (self.to_nxt, self.to_prev, self.to_nxt, self.to_prev)[kind]),
                device_id_type=pl.DeviceIdType.MESH,
            )

        def fill(self, slot):
            buf, place = (
                (self.own, 0), (self.nxt, 1), (self.prev, 3), (self.far, 2)
            )[slot]
            source = self.grid(lax.rem(self.me + place, 4), self.swap_me)
            for step in (2, 1, 3):
                owner = self.grid(self.me, lax.rem(self.swap_me + step, 4))
                self.pack[step - 1, slot] = buf[item_for(source, owner)]
            self.got[0, slot] = buf[item_for(source, g)]

        def swap(self, group, kind):
            slots = (pl.ds(0, 1), pl.ds(1, 2), pl.ds(3, 1))[group]
            top, low = pl.ds(0, SPLIT // 2), pl.ds(SPLIT // 2, SPLIT // 2)
            src, dst, device = (
                (self.pack.at[1, slots, top], self.passed.at[0, slots], self.swap_nxt),
                (self.pack.at[1, slots, low], self.passed.at[1, slots], self.swap_prev),
                (self.pack.at[0, slots], self.got.at[3, slots], self.swap_nxt),
                (self.pack.at[2, slots], self.got.at[1, slots], self.swap_prev),
                (self.passed.at[0, slots], self.got.at[2, slots, top], self.swap_nxt),
                (self.passed.at[1, slots], self.got.at[2, slots, low], self.swap_prev),
            )[kind]
            slot = 6 * (3 * self.base + group) + kind
            return pltpu.make_async_remote_copy(
                src_ref=src, dst_ref=dst,
                send_sem=swap_send.at[slot], recv_sem=swap_recv.at[slot],
                device_id=(r, device), device_id_type=pl.DeviceIdType.MESH,
            )

    along_x = Way(line_x, gx, x_prev, x_next, gz, z_prev, z_next, True, (pack_x, pass_x, got_x), 0)
    along_z = Way(line_z, gz, z_prev, z_next, gx, x_prev, x_next, False, (pack_z, pass_z, got_z), 1)
    ways = (along_x, along_z)

    def pass_on(k):
        for way in ways:
            way.line_copy(0, k).wait_recv()
            way.line_copy(2, k).start()
            way.line_copy(1, k).wait_recv()
            way.line_copy(3, k).start()

    def swap_out(group, slots):
        for way in ways:
            for slot in slots:
                way.fill(slot)
        for kind in range(4):
            for way in ways:
                way.swap(group, kind).start()

    def swap_on(group):
        for kind in range(2):
            for way in ways:
                way.swap(group, kind).wait_recv()
                way.swap(group, kind + 4).start()

    def sign(k, carry):
        pick_blocks(k, h_far_b, y_far, (1,))
        norm = jnp.zeros((1, TILE), jnp.float32)
        for n in range(3):
            cols = slice(n * TILE, (n + 1) * TILE)
            part = jnp.dot(
                lhs[:, :TILE], rhs[:TILE, cols], preferred_element_type=jnp.float32
            )
            mat = (total[k, :, cols] + part).astype(jnp.bfloat16).astype(jnp.float32)
            shifted = mat - jnp.where(eye_like(ORDER, TILE, -n * TILE), mu, 0.0)
            norm += jnp.sum(shifted * shifted, axis=0, keepdims=True)
            w[:, cols] = shifted.astype(jnp.bfloat16)
        square_scale = jnp.sum(norm, axis=1, keepdims=True) / ORDER + 1e-06
        scale_y = 0.25 / square_scale
        scale_z = 0.25 / jnp.sqrt(square_scale)
        for n in range(3):
            cols = slice(n * TILE, (n + 1) * TILE)
            square = jnp.dot(w[...], w[:, cols], preferred_element_type=jnp.float32)
            diag = jnp.where(eye_like(ORDER, TILE, -n * TILE), 3.0, 0.0)
            y0[:, cols] = (diag - scale_y * square).astype(jnp.bfloat16)
        for n in range(3):
            cols = slice(n * TILE, (n + 1) * TILE)
            step = jnp.dot(w[...], y0[:, cols], preferred_element_type=jnp.float32)
            z1[:, cols] = (scale_z * step).astype(jnp.bfloat16)
        @pl.when(k > 0)
        def _():
            pass_on(k - 1)

        square = jnp.dot(z1[...], z1[:, :BLK], preferred_element_type=jnp.float32)
        eye = eye_like(ORDER, BLK, 0)
        y1[...] = (jnp.where(eye, 3.0, 0.0) - square).astype(jnp.bfloat16)
        last = 0.5 * jnp.dot(z1[...], y1[...], preferred_element_type=jnp.float32)
        columns = (0.5 * (jnp.where(eye, 1.0, 0.0) - last)).astype(jnp.bfloat16)
        along_x.own[k] = columns[:SPLIT]
        along_z.own[k] = columns[SPLIT:]
        for way in ways:
            way.line_copy(0, k).start()
            way.line_copy(1, k).start()

        return carry

    lax.fori_loop(0, SUB_DEV, sign, 0)
    swap_out(0, (0,))
    pass_on(SUB_DEV - 1)
    swap_out(1, (1, 2))
    swap_on(0)
    for k in range(SUB_DEV):
        for way in ways:
            way.line_copy(2, k).wait_recv()
            way.line_copy(3, k).wait_recv()
    swap_out(2, (3,))
    swap_on(1)
    swap_on(2)
    for group in range(3):
        for kind in range(2, 6):
            for way in ways:
                way.swap(group, kind).wait_recv()
    phi_copy.wait()

    def slot_of(place):
        return place + (place == 2).astype(jnp.int32) - (place == 3).astype(jnp.int32)

    across = (((0,), (0,)), ((), ()))
    window = jnp.zeros((1, EXT), jnp.float32)
    for t in range(OWN_MAX):
        from_z = slot_source[t] // 4
        from_x = lax.rem(slot_source[t] - 4 * from_z + 4 - gx, 4)
        from_z = lax.rem(from_z + 4 - gz, 4)
        column[:SPLIT] = got_x[from_z, slot_of(from_x)]
        column[SPLIT:] = got_z[from_x, slot_of(from_z)]
        proj = lax.dot_general(column[...], phi[t], across, preferred_element_type=jnp.float32)
        values = jnp.sum(proj * phi[t, :BLK].astype(jnp.float32), axis=0, keepdims=True)
        window += values * (count > t).astype(jnp.int32).astype(jnp.float32)
    for i in range(EXT // BLK):
        pieces[i] = window[:, i * BLK : (i + 1) * BLK]

    def give(slot, piece, place, row, grid):
        copy = pltpu.make_async_remote_copy(
            src_ref=pieces.at[piece], dst_ref=sums.at[place],
            send_sem=sum_send.at[slot], recv_sem=sum_recv.at[place],
            device_id=(row, grid), device_id_type=pl.DeviceIdType.MESH,
        )
        copy.start()
        return copy

    given = []
    for row in range(2):
        given.append(give(7 + row, 10 + row, 8 + r, row, brick_next))
        given.append(give(9 + row, row, 8 + r, 6 + row, brick_prev))
    for step in range(1, 8):
        row = lax.rem(r + step, 8)
        given.append(give(step - 1, 2 + row, r, row, g))
    sums[r] = pieces[2 + r]

    def arrived(place):
        pltpu.make_async_copy(sums.at[place], sums.at[place], sum_recv.at[place]).wait()

    for step in range(1, 8):
        arrived(lax.rem(r + step, 8))

    @pl.when((r < 2) | (r >= 6))
    def _():
        for row in range(8):
            arrived(8 + row)

    out[...] = jnp.sum(sums[...], axis=0)
    for copy in (*copies.values(), *given):
        copy.wait_send()
    for way in ways:
        for kind in range(4):
            for k in range(SUB_DEV):
                way.line_copy(kind, k).wait_send()
        for kind in range(6):
            for group in range(3):
                way.swap(group, kind).wait_send()


def region(h_rows, x_blocks, x_cols, picks, owners, mu, orbitals):
    vmem = pl.BlockSpec(memory_space=pltpu.VMEM)
    smem = pl.BlockSpec(memory_space=pltpu.SMEM)
    hbm = pl.BlockSpec(memory_space=pl.ANY)
    h_buf = pltpu.VMEM((2, KB, 2 * BLK, BLK), jnp.bfloat16)
    h_far = pltpu.VMEM((2, KB, BLK, BLK), jnp.bfloat16)
    square = pltpu.VMEM((ORDER, ORDER), jnp.bfloat16)
    columns = pltpu.VMEM((ORDER, BLK), jnp.bfloat16)
    line = [pltpu.VMEM((SUB_DEV, SPLIT, BLK), jnp.bfloat16)] * 4
    pack = pltpu.VMEM((3, 4, SPLIT, BLK), jnp.bfloat16)
    slots4 = pltpu.VMEM((4, 4, SPLIT, BLK), jnp.bfloat16)
    passed = pltpu.VMEM((2, 4, SPLIT // 2, BLK), jnp.bfloat16)
    dma = pltpu.SemaphoreType.DMA
    return pl.pallas_call(
        region_kernel,
        out_shape=jax.ShapeDtypeStruct((1, BLK), jnp.float32),
        in_specs=[hbm, vmem, smem, smem, smem, smem, hbm],
        out_specs=vmem,
        scratch_shapes=[
            h_buf, h_buf, h_buf, h_far, h_far,
            pltpu.VMEM((KB, NZ + 1, BLK, BLK), jnp.bfloat16),
            pltpu.VMEM((KB, 8, BLK), jnp.int32),
            pltpu.SMEM((KB, 8, BLK), jnp.int32),
            pltpu.VMEM((ORDER, 4 * BLK), jnp.bfloat16),
            pltpu.VMEM((4 * BLK, ORDER), jnp.bfloat16),
            pltpu.VMEM((SUB_DEV, ORDER, ORDER), jnp.float32),
            square, square, square, columns,
            pltpu.VMEM((OWN_MAX, ORDER, EXT), jnp.bfloat16),
            line, line, pack, pack, passed, passed, slots4, slots4, columns,
            pltpu.VMEM((EXT // BLK, 1, BLK), jnp.float32),
            pltpu.VMEM((16, 1, BLK), jnp.float32),
            dma((N_SEM,)), dma((N_SEM,)), dma, dma, dma,
            dma((8, SUB_DEV)), dma((8, SUB_DEV)), dma((36,)), dma((36,)), dma((11,)), dma((16,)),
        ],
        compiler_params=pltpu.CompilerParams(
            collective_id=0, has_side_effects=True, vmem_limit_bytes=60 << 20
        ),
        name="region",
    )(h_rows, x_blocks, x_cols, picks, owners, mu, orbitals)


def on_device(h_rows, x_blocks, x_cols, sub_blocks, owners, shift_mu, orbitals):
    return region(
        h_rows[0], x_blocks[0], x_cols[0], jnp.transpose(sub_blocks[0], (1, 0, 2)),
        jnp.transpose(owners, (2, 0, 1)), shift_mu.reshape(1, 1), orbitals[0, 0],
    )


def solution(mesh):
    in_specs = (
        P("grid", "row", None),
        P("grid", "row", None, None, None),
        P("grid", "row", None),
        P("row", "grid", None, None),
        P("row", None, None),
        P(),
        P("row", "grid", None, None, None),
    )
    out_specs = P("grid", "row")
    return jax.shard_map(
        on_device, mesh=mesh, in_specs=in_specs, out_specs=out_specs, check_vma=False
    )
```
